128 devices in a mesh: head: 4 (over x), ctx: 32 (over z, y, core).
Axes of the slice: x: 4, y: 4, z: 4, core: 2. Of those that a mesh axis runs over, the one named last changes fastest.
Arguments:
- queries: bfloat16 [16384, 4096], P('ctx', 'head'), may hold values from -4 to 4
- key_input: bfloat16 [16384, 4096], P('ctx', 'head'), may hold values from -4 to 4
- value_input: bfloat16 [16384, 4096], P('ctx', 'head'), may hold values from -32 to 32
- norm_gain: float32 [4096], P('head'), may hold values from 0.1 to 1.9
- out_grad: bfloat16 [16384, 4096], P('ctx', 'head'), may hold values from -6 to 6
- doc_lengths: int32 [8], replicated, may hold values from 1 to 64, 128 in all
Outputs:
- normed_out: bfloat16 [16384, 4096], P('ctx', 'head')
- query_grad: bfloat16 [16384, 4096], P('ctx', 'head')
- key_grad: bfloat16 [16384, 4096], P('ctx', 'head')
- value_grad: bfloat16 [16384, 4096], P('ctx', 'head')
The draws below stay inside these ranges and needn't reach their ends.
Inputs may be any that keep to these rules, and one draw needn't show every extreme that they name: `doc_lengths`: the lengths of the slab's 8 documents in order, in units of 128 tokens; they sum to 128, and the longest has exactly 64.
All inputs are finite; a program needn't handle non-finite values.
Results may differ from the reference program's by a relative error of at most 0.0053.
Values sent between devices are 32-bit elements; how exact they have to be, the bound alone decides.
No kernel may reach another device: no remote copies, remote signals or barrier semaphores. Data moves between devices by JAX's collectives and lax.ppermute only.
A program may use at most 128 MiB of HBM per device.

```python
import math
import jax
import jax.numpy as jnp
import numpy as np
from jax import lax

HEADS = 32
HEAD_DIM = 128
BLOCK = 512
GRAIN = 128
TOKENS = 16384
NDOCS = 8
MOST_GRAINS = 64


def draw_value_input(key, part):
    key_base, key_column, key_token = jax.random.split(key, 3)
    width_all = HEADS * HEAD_DIM
    head_place = (jnp.arange(width_all) // HEAD_DIM).astype(jnp.float32) / max(HEADS - 1, 1)
    base = jnp.clip(jax.random.normal(key_base, (TOKENS, width_all), jnp.float32), -4.0, 4.0)
    rising = jnp.exp(jnp.log(3.0) * head_place)
    column_scale = jnp.exp(jax.random.uniform(key_column, (width_all,), jnp.float32, 0.0, jnp.log(4.0))) * rising
    token_scale = jnp.exp(jax.random.uniform(key_token, (TOKENS, 1), jnp.float32, 0.0, jnp.log(4.0)))
    return (base * column_scale[None, :] * token_scale * 0.125).astype(jnp.bfloat16)


def level_of(own_key, dims, shards, least, top_value):
    def one(axis_at, shards_of):
        steps = jax.random.uniform(jax.random.fold_in(jax.random.fold_in(own_key, 6), axis_at), (shards_of,), jnp.float32, least / len(shards), top_value / len(shards))
        return jnp.repeat(jnp.exp(steps), dims[axis_at] // shards_of).reshape((-1,) + (1,) * (len(dims) - axis_at - 1))

    loudness = one(*shards[0])
    for cut in shards[1:]:
        loudness = loudness * one(*cut)
    return loudness


def length_profile(number_of, total, most, slope):
    weights = [(1 << 20) // math.isqrt(grade ** slope) + 1 for grade in range(2, number_of + 1)]
    spare, counts = total - most - (number_of - 1), [1] * (number_of - 1)
    while spare > 0:
        movable = [i for i in range(number_of - 1) if counts[i] < most]
        pool, remaining = sum([weights[i] for i in movable]), spare
        for i in movable:
            addition = min(most - counts[i], max(1, remaining * weights[i] // pool), spare)
            counts[i] = counts[i] + addition
            spare = spare - addition
    return np.array([most] + counts)


def uneven_parts(own_key, number_of, total, most, slope):
    if number_of == 2:
        one = jax.random.randint(own_key, (), max(1, total - most), min(most, total - 1) + 1)
        return jnp.stack([one, total - one])
    sizes = jnp.asarray(length_profile(number_of, total, most, slope), jnp.int32)
    twos = (number_of - 1) // 2
    giver, sink = sizes[1:1 + 2 * twos:2], sizes[2:2 + 2 * twos:2]
    room = jnp.minimum(giver - 1, most - sink)
    moved = jax.random.randint(jax.random.fold_in(own_key, 1), (twos,), 0, 1 << 20) % (room + 1)
    sizes = sizes.at[1:1 + 2 * twos:2].set(giver - moved).at[2:2 + 2 * twos:2].set(sink + moved)
    return sizes[jax.random.permutation(jax.random.fold_in(own_key, 2), number_of)]


def bell_draw(own_key, extent, width, most, pieces=(), kind=jnp.bfloat16):
    result = width * jax.random.normal(own_key, extent, jnp.float32)
    if pieces:
        result = result * level_of(own_key, extent, pieces, -0.22, 0.18)
    return jnp.clip(result, -most, most).astype(kind)


def setup_inputs(seed: int = 0) -> dict:
    keys = jax.random.split(jax.random.key(seed), 7)
    queries = bell_draw(keys[0], (TOKENS, HEADS * HEAD_DIM), 1.0, 4.0, ((0, 32), (1, 4)))
    key_input = bell_draw(keys[1], (TOKENS, HEADS * HEAD_DIM), 1.0, 4.0, ((0, 32), (1, 4)))
    value_input = draw_value_input(jax.random.fold_in(keys[6], 71), 0)
    norm_gain = jnp.clip(1.0 + 0.18 * jax.random.normal(keys[3], (HEADS * HEAD_DIM,), jnp.float32), 0.1, 1.9)
    out_grad = bell_draw(keys[4], (TOKENS, HEADS * HEAD_DIM), 1.0, 6.0, ((0, 32), (1, 4)))
    doc_lengths = uneven_parts(keys[5], NDOCS, TOKENS // GRAIN, MOST_GRAINS, 2).astype(jnp.int32)
    return {"queries": queries, "key_input": key_input, "value_input": value_input, "norm_gain": norm_gain, "out_grad": out_grad, "doc_lengths": doc_lengths}


EPSILON = 1e-06

def doc_index(starts_at, grain_ids, total_grains):
    counted = lax.optimization_barrier(jnp.sum((starts_at[None, :] <= grain_ids[:, None]).astype(jnp.int32), axis=1, dtype=jnp.int32))
    return (counted - 1 + (grain_ids >= total_grains).astype(jnp.int32)).astype(jnp.int32)

def reference(queries, key_input, value_input, norm_gain, out_grad, doc_lengths):
    width_all = HEADS * HEAD_DIM
    count_blocks = TOKENS // BLOCK
    total_grains = TOKENS // GRAIN
    highest = lax.Precision.HIGHEST
    starts_at = (jnp.cumsum(doc_lengths, dtype=jnp.int32) - doc_lengths).astype(jnp.int32)
    token_docs = doc_index(starts_at, jnp.arange(TOKENS, dtype=jnp.int32) // GRAIN, total_grains)
    block_shape = (count_blocks, BLOCK, HEADS, HEAD_DIM)
    query_all = queries.reshape(block_shape)
    key_all = key_input.reshape(block_shape)
    value_all = value_input.reshape(block_shape)
    grad_all = out_grad.reshape(count_blocks, BLOCK, width_all)
    docs_all = token_docs.reshape(count_blocks, BLOCK)
    causal = jnp.arange(BLOCK)[:, None] >= jnp.arange(BLOCK)[None, :]

    def masked_round(values_in, seg_docs):
        allowed = causal & (seg_docs[:, None] == seg_docs[None, :])
        rounded = jnp.where(allowed[None], values_in, 0.0).astype(jnp.bfloat16)
        return lax.optimization_barrier(rounded).astype(jnp.float32)

    def forward_step(running, inputs):
        state_sum, previous = running
        query_block, key_block, value_block, grad_block, seg_docs = inputs
        query_f = query_block.astype(jnp.float32)
        key_f = key_block.astype(jnp.float32)
        value_f = value_block.astype(jnp.float32)
        weights = masked_round(jnp.einsum('ihd,jhd->hij', query_f, key_f), seg_docs)
        follows = (seg_docs == previous).astype(jnp.float32)
        mixed_part = jnp.einsum('hij,jhe->ihe', weights, value_f)
        mixed_part = mixed_part + follows[:, None, None] * jnp.einsum('ihd,hde->ihe', query_f, state_sum, precision=highest)
        flat_mixed = mixed_part.reshape(BLOCK, width_all)
        root_mean = jnp.sqrt(lax.optimization_barrier(jnp.mean(flat_mixed * flat_mixed, axis=1)) + EPSILON)[:, None]
        normed = flat_mixed / root_mean
        normed_out = (normed * norm_gain[None, :]).astype(jnp.bfloat16)
        scaled_grad = norm_gain[None, :] * grad_block.astype(jnp.float32)
        dot_mean = lax.optimization_barrier(jnp.mean(normed * scaled_grad, axis=1))[:, None]
        grad_mixed = ((scaled_grad - normed * dot_mean) / root_mean).astype(jnp.bfloat16)
        last_doc = seg_docs[-1]
        tail_mask = (seg_docs == last_doc).astype(jnp.float32)
        new_state = jnp.where(last_doc == previous, state_sum, 0.0)
        new_state = new_state + jnp.einsum('jhd,jhe->hde', key_f * tail_mask[:, None, None], value_f)
        return ((new_state, last_doc), (normed_out, grad_mixed, state_sum, previous))
    start_state = (jnp.zeros((HEADS, HEAD_DIM, HEAD_DIM), jnp.float32), jnp.int32(-1))
    _, (normed_all, grad_mixed_all, states_all, previous_all) = lax.scan(forward_step, start_state, (query_all, key_all, value_all, grad_all, docs_all))

    def backward_step(running, inputs):
        upper_sum, following = running
        query_block, key_block, value_block, grad_block, seg_docs, state_sum, previous = inputs
        query_f = query_block.astype(jnp.float32)
        key_f = key_block.astype(jnp.float32)
        value_f = value_block.astype(jnp.float32)
        grad_f = grad_block.astype(jnp.float32).reshape(BLOCK, HEADS, HEAD_DIM)
        weights = masked_round(jnp.einsum('ihd,jhd->hij', query_f, key_f), seg_docs)
        grad_weights = masked_round(jnp.einsum('ihe,jhe->hij', grad_f, value_f), seg_docs)
        follows = (seg_docs == previous).astype(jnp.float32)[:, None, None]
        leads_into = (seg_docs == following).astype(jnp.float32)[:, None, None]
        query_grad = jnp.einsum('hij,jhd->ihd', grad_weights, key_f)
        query_grad = query_grad + follows * jnp.einsum('hde,ihe->ihd', state_sum, grad_f, precision=highest)
        key_grad = jnp.einsum('hij,ihd->jhd', grad_weights, query_f)
        key_grad = key_grad + leads_into * jnp.einsum('hde,jhe->jhd', upper_sum, value_f, precision=highest)
        value_grad = jnp.einsum('hij,ihe->jhe', weights, grad_f)
        value_grad = value_grad + leads_into * jnp.einsum('hde,jhd->jhe', upper_sum, key_f, precision=highest)
        first_doc = seg_docs[0]
        head_mask = (seg_docs == first_doc).astype(jnp.float32)
        new_upper = jnp.where(first_doc == following, upper_sum, 0.0)
        new_upper = new_upper + jnp.einsum('ihd,ihe->hde', query_f * head_mask[:, None, None], grad_f)
        outputs = (query_grad.reshape(BLOCK, width_all).astype(jnp.bfloat16), key_grad.reshape(BLOCK, width_all).astype(jnp.bfloat16), value_grad.reshape(BLOCK, width_all).astype(jnp.bfloat16))
        return ((new_upper, first_doc), outputs)
    end_state = (jnp.zeros((HEADS, HEAD_DIM, HEAD_DIM), jnp.float32), jnp.int32(NDOCS))
    _, (query_grads, key_grads, value_grads) = lax.scan(backward_step, end_state, (query_all, key_all, value_all, grad_mixed_all, docs_all, states_all, previous_all), reverse=True)
    return (normed_all.reshape(TOKENS, width_all), query_grads.reshape(TOKENS, width_all), key_grads.reshape(TOKENS, width_all), value_grads.reshape(TOKENS, width_all))
```

```python
import jax
import jax.numpy as jnp
from jax import lax
from jax.sharding import PartitionSpec as P

HEADS = 32
HEAD_DIM = 128
BLOCK = 512
GRAIN = 128


EPSILON = 1e-06


def prefix(part, axis, combine, identity, reverse):
    count = lax.axis_size(axis)
    place = lax.axis_index(axis)
    ahead = count - 1 - place if reverse else place
    gathered = jax.tree.map(lambda a: lax.all_gather(a, axis), part)
    state = jax.tree.map(lambda a, e: jnp.zeros_like(a) + jnp.asarray(e, a.dtype), part, identity)

    def one(lap, state):
        source = count - 1 - lap if reverse else lap
        return combine(
            state, jax.tree.map(lambda a: lax.dynamic_index_in_dim(a, source, 0, False), gathered)
        )

    return lax.fori_loop(0, ahead, one, state)


def doc_index(starts_at, grain_ids, total_grains):
    counted = jnp.sum(
        (starts_at[None, :] <= grain_ids[:, None]).astype(jnp.int32), axis=1, dtype=jnp.int32
    )
    return counted - 1 + (grain_ids >= total_grains).astype(jnp.int32)


def join_reset(earlier, nearer):
    return (jnp.maximum(earlier[0], nearer[0]), nearer[1] + (1.0 - nearer[0]) * earlier[1])


def masked_round(values_in, allowed):
    return jnp.where(allowed[None], values_in, 0.0).astype(jnp.bfloat16)


def on_device(queries, key_input, value_input, norm_gain, out_grad, doc_lengths):
    highest = lax.Precision.HIGHEST
    rows_here = queries.shape[0]
    width_here = queries.shape[1]
    heads_here = width_here // HEAD_DIM
    width_all = HEADS * HEAD_DIM
    grains_here = rows_here // GRAIN
    blocks_here = rows_here // BLOCK
    ctx_count = lax.axis_size("ctx")
    total_grains = ctx_count * grains_here
    device = lax.axis_index("ctx")
    first_grain = device * grains_here
    slots = jnp.arange(doc_lengths.shape[0])
    starts_at = jnp.sum(
        jnp.where(slots[None, :] < slots[:, None], doc_lengths[None, :], 0), axis=1, dtype=jnp.int32
    )
    token_docs = doc_index(
        starts_at, first_grain + jnp.arange(rows_here, dtype=jnp.int32) // GRAIN, total_grains
    )
    edge_grains = jnp.stack([first_grain - 1, first_grain + grains_here])
    edge_docs = doc_index(starts_at, edge_grains, total_grains)
    before_doc = edge_docs[0]
    after_doc = edge_docs[1]
    query_heads = queries.reshape(rows_here, heads_here, HEAD_DIM)
    key_heads = key_input.reshape(rows_here, heads_here, HEAD_DIM)
    value_heads = value_input.reshape(rows_here, heads_here, HEAD_DIM)
    causal = jnp.arange(BLOCK)[:, None] >= jnp.arange(BLOCK)[None, :]
    state_sum = jnp.zeros((heads_here, HEAD_DIM, HEAD_DIM), jnp.float32)
    query_block = query_heads
    key_block = key_heads
    value_block = value_heads
    seg_docs = token_docs
    allowed = causal & (seg_docs[:, None] == seg_docs[None, :])
    scores = jnp.einsum("ihd,jhd->hij", query_block, key_block, preferred_element_type=jnp.float32)
    weights = masked_round(scores, allowed)
    local_parts = [
        jnp.einsum("hij,jhe->ihe", weights, value_block, preferred_element_type=jnp.float32)
    ]
    entry_states = [state_sum]
    entry_docs = [before_doc]
    weights_kept = [weights]
    masks_kept = [allowed]
    last_doc = seg_docs[-1]
    tail_keys = key_block * (seg_docs == last_doc).astype(jnp.bfloat16)[:, None, None]
    state_sum = jnp.where(last_doc == before_doc, state_sum, 0.0) + jnp.einsum(
        "jhd,jhe->hde", tail_keys, value_block, preferred_element_type=jnp.float32
    )
    forward_flag = (token_docs[-1] != before_doc).astype(jnp.float32).reshape(1)
    incoming = prefix(
        (forward_flag, state_sum),
        "ctx",
        join_reset,
        (jnp.zeros((1,), jnp.float32), jnp.zeros_like(state_sum)),
        False,
    )[1]
    segment = 0
    entry_total = (
        entry_states[segment] + jnp.where(entry_docs[segment] == before_doc, 1.0, 0.0) * incoming
    )
    entry_totals = [entry_total]
    follows = (token_docs == entry_docs[segment]).astype(jnp.float32)
    mixed_parts = local_parts[segment] + follows[:, None, None] * jnp.einsum(
        "ihd,hde->ihe", query_heads.astype(jnp.float32), entry_total, precision=highest
    )
    flat_mixed = mixed_parts.reshape(rows_here, width_here)
    scaled_grad = norm_gain[None, :] * out_grad.astype(jnp.float32)
    square_sum = lax.psum(jnp.sum(flat_mixed * flat_mixed, axis=1), "head")
    root_mean = jnp.sqrt(square_sum / width_all + EPSILON)
    normed = flat_mixed / root_mean[:, None]
    dot_mean = lax.psum(jnp.sum(normed * scaled_grad, axis=1), "head") / width_all
    normed_out = (normed * norm_gain[None, :]).astype(jnp.bfloat16)
    grad_mixed = ((scaled_grad - normed * dot_mean[:, None]) / root_mean[:, None]).astype(
        jnp.bfloat16
    )
    grad_heads = grad_mixed.reshape(rows_here, heads_here, HEAD_DIM)
    upper_sum = jnp.zeros((heads_here, HEAD_DIM, HEAD_DIM), jnp.float32)
    following = after_doc
    query_parts = [None] * blocks_here
    key_parts = [None] * blocks_here
    value_parts = [None] * blocks_here
    upper_states = [None] * blocks_here
    upper_docs = [None] * blocks_here
    for segment in reversed(range(blocks_here)):
        query_block = query_heads
        key_block = key_heads
        value_block = value_heads
        seg_docs = token_docs
        grad_scores = jnp.einsum(
            "ihe,jhe->hij", grad_heads, value_block, preferred_element_type=jnp.float32
        )
        grad_weights = masked_round(grad_scores, masks_kept[segment])
        follows = (seg_docs == entry_docs[segment]).astype(jnp.float32)[:, None, None]
        query_part = jnp.einsum(
            "hij,jhd->ihd", grad_weights, key_block, preferred_element_type=jnp.float32
        )
        query_parts[segment] = query_part + follows * jnp.einsum(
            "hde,ihe->ihd", entry_totals[segment], grad_heads.astype(jnp.float32), precision=highest
        )
        key_parts[segment] = jnp.einsum(
            "hij,ihd->jhd", grad_weights, query_block, preferred_element_type=jnp.float32
        )
        value_parts[segment] = jnp.einsum(
            "hij,ihe->jhe", weights_kept[segment], grad_heads, preferred_element_type=jnp.float32
        )
        upper_states[segment] = upper_sum
        upper_docs[segment] = following
        first_doc = seg_docs[0]
        head_queries = query_block * (seg_docs == first_doc).astype(jnp.bfloat16)[:, None, None]
        upper_sum = jnp.where(first_doc == following, upper_sum, 0.0) + jnp.einsum(
            "ihd,ihe->hde", head_queries, grad_heads, preferred_element_type=jnp.float32
        )
        following = first_doc
    backward_flag = (token_docs[0] != after_doc).astype(jnp.float32).reshape(1)
    suffix_in = prefix(
        (backward_flag, upper_sum),
        "ctx",
        join_reset,
        (jnp.zeros((1,), jnp.float32), jnp.zeros_like(upper_sum)),
        True,
    )[1]
    segment = 0
    upper_total = (
        upper_states[segment] + jnp.where(upper_docs[segment] == after_doc, 1.0, 0.0) * suffix_in
    )
    leads_into = (token_docs == upper_docs[segment]).astype(jnp.float32)[:, None, None]
    key_final = key_parts[segment] + leads_into * jnp.einsum(
        "hde,jhe->jhd", upper_total, value_heads.astype(jnp.float32), precision=highest
    )
    value_final = value_parts[segment] + leads_into * jnp.einsum(
        "hde,jhd->jhe", upper_total, key_heads.astype(jnp.float32), precision=highest
    )
    query_grad = query_parts[0].reshape(rows_here, width_here).astype(jnp.bfloat16)
    key_grad = key_final.reshape(rows_here, width_here).astype(jnp.bfloat16)
    value_grad = value_final.reshape(rows_here, width_here).astype(jnp.bfloat16)
    return (normed_out, query_grad, key_grad, value_grad)


def solution(mesh):
    in_specs = (
        P("ctx", "head"),
        P("ctx", "head"),
        P("ctx", "head"),
        P("head"),
        P("ctx", "head"),
        P(),
    )
    out_specs = (P("ctx", "head"), P("ctx", "head"), P("ctx", "head"), P("ctx", "head"))
    return jax.shard_map(
        on_device, mesh=mesh, in_specs=in_specs, out_specs=out_specs, check_vma=False
    )
```

```python
import jax
import jax.numpy as jnp
from jax import lax
from jax.experimental import pallas as pl
from jax.experimental.pallas import tpu as pltpu
from jax.sharding import PartitionSpec as P

HEADS = 32
HEAD_DIM = 128
BLOCK = 512
GRAIN = 128
NDOCS = 8
GRAINS = BLOCK // GRAIN
WIDTH = HEADS * HEAD_DIM
HALF = BLOCK // 2
EPSILON = 1e-06

F32 = jnp.float32
BF16 = jnp.bfloat16


def dot(a, b, dims):
    return lax.dot_general(a, b, (dims, ((), ())), preferred_element_type=F32)


NN = ((1,), (0,))
NT = ((1,), (1,))
TN = ((0,), (0,))


def grain_docs(lengths_ref):
    total = lax.axis_size("ctx") * GRAINS
    first = lax.axis_index("ctx") * GRAINS
    starts = [jnp.int32(0)]
    for i in range(NDOCS - 1):
        starts.append(starts[-1] + lengths_ref[i])
    docs = []
    for k in range(-1, GRAINS + 1):
        grain = first + k
        count = (grain >= total).astype(jnp.int32) - 1
        for s in starts:
            count = count + (s <= grain).astype(jnp.int32)
        docs.append(count)
    return docs


def rows_equal(docs, doc, cols, dtype):
    parts = [
        jnp.full((GRAIN, cols), (docs[1 + g] == doc).astype(F32), F32) for g in range(GRAINS)
    ]
    return jnp.concatenate(parts, axis=0).astype(dtype)


def pair_mask(docs):
    rows = lax.broadcasted_iota(jnp.int32, (GRAIN, GRAIN), 0)
    cols = lax.broadcasted_iota(jnp.int32, (GRAIN, GRAIN), 1)
    lower = jnp.where(rows >= cols, 1.0, 0.0).astype(F32)
    out = []
    for i in range(GRAINS):
        line = []
        for j in range(GRAINS):
            if j < i:
                same = (docs[1 + i] == docs[1 + j]).astype(F32)
                line.append(jnp.full((GRAIN, GRAIN), same, F32))
            elif j == i:
                line.append(lower)
            else:
                line.append(jnp.zeros((GRAIN, GRAIN), F32))
        out.append(jnp.concatenate(line, axis=1))
    return jnp.concatenate(out, axis=0).astype(BF16)


def split_rows(x):
    high = x.astype(BF16)
    low = (x - high.astype(F32)).astype(BF16)
    return jnp.concatenate([high, low], axis=0)


def split_cols(x):
    high = x.astype(BF16)
    low = (x - high.astype(F32)).astype(BF16)
    return jnp.concatenate([high, low], axis=1)


def twice(x):
    return jnp.concatenate([x, x], axis=1)


def head_cols(h):
    return slice(h * HEAD_DIM, (h + 1) * HEAD_DIM)


STEP_HEADS = 2
STEP_COLS = STEP_HEADS * HEAD_DIM


def state_kernel(lengths_ref, key_ref, value_ref, out_ref):
    docs = grain_docs(lengths_ref)
    mask = rows_equal(docs, docs[GRAINS], HEAD_DIM, BF16)
    for h in range(STEP_HEADS):
        keys = key_ref[:, head_cols(h)] * mask
        out_ref[h * HEAD_DIM : (h + 1) * HEAD_DIM, :] = dot(keys, value_ref[:, head_cols(h)], TN)


def local_kernel(lengths_ref, query_ref, key_ref, value_ref, out_ref, mask_ref):
    @pl.when(pl.program_id(0) == 0)
    def _():
        mask_ref[...] = pair_mask(grain_docs(lengths_ref))

    for h in range(STEP_HEADS):
        cols = head_cols(h)
        for r in range(2):
            rows = slice(r * HALF, (r + 1) * HALF)
            upto = (r + 1) * HALF
            weights = dot(query_ref[rows, cols], key_ref[:upto, cols], NT).astype(BF16)
            weights = weights * mask_ref[rows, :upto]
            out_ref[rows, cols] = dot(weights, value_ref[:upto, cols], NN)


def scan_kernel(lengths_ref, parts_ref, out_ref, keep_ref, *, backward):
    count = parts_ref.shape[0]
    for b in range(count):
        keep_ref[b] = jnp.int32(1)
    start = jnp.int32(0)
    for i in range(NDOCS - 1):
        start = start + lengths_ref[i]
        place = (start - 1) // GRAINS if backward else start // GRAINS
        keep_ref[place] = jnp.int32(0)
    running = jnp.zeros(parts_ref.shape[1:], F32)
    for b in reversed(range(count)) if backward else range(count):
        out_ref[b] = running
        running = parts_ref[b] + keep_ref[b].astype(F32) * running


def mixed_kernel(
    lengths_ref, query_ref, local_ref, state_ref, grad_ref, gain_ref, mixed_ref, sums_ref, acc_ref
):
    step = pl.program_id(0)
    docs = grain_docs(lengths_ref)
    mask = rows_equal(docs, docs[0], HEAD_DIM, BF16)
    squares = jnp.zeros((BLOCK, HEAD_DIM), F32)
    dots = jnp.zeros((BLOCK, HEAD_DIM), F32)
    for h in range(STEP_HEADS):
        cols = head_cols(h)
        state = split_rows(state_ref[h * HEAD_DIM : (h + 1) * HEAD_DIM, :])
        mixed = local_ref[:, cols] + dot(twice(query_ref[:, cols] * mask), state, NN)
        mixed_ref[:, cols] = mixed
        squares = squares + mixed * mixed
        dots = dots + mixed * (gain_ref[:, cols] * grad_ref[:, cols].astype(F32))

    @pl.when(step == 0)
    def _():
        acc_ref[0] = squares
        acc_ref[1] = dots

    @pl.when(step > 0)
    def _():
        acc_ref[0] += squares
        acc_ref[1] += dots

    @pl.when(step == pl.num_programs(0) - 1)
    def _():
        for n in range(2):
            sums_ref[n : n + 1, :] = jnp.sum(acc_ref[n].T, axis=0, keepdims=True)


def grad_kernel(
    lengths_ref,
    sums_ref,
    sums1_ref,
    sums2_ref,
    sums3_ref,
    mixed_ref,
    grad_ref,
    gain_ref,
    query_ref,
    normed_ref,
    grad_mixed_ref,
    upper_ref,
    scale_ref,
):
    @pl.when(pl.program_id(0) == 0)
    def _():
        total = sums_ref[...] + sums1_ref[...] + sums2_ref[...] + sums3_ref[...]
        root = jnp.sqrt(total[0:1, :] / WIDTH + EPSILON)
        inverse = 1.0 / root
        dots = total[1:2, :] * inverse / WIDTH
        scale_ref[0] = jnp.broadcast_to(inverse, (HEAD_DIM, BLOCK)).T
        scale_ref[1] = jnp.broadcast_to(dots, (HEAD_DIM, BLOCK)).T

    docs = grain_docs(lengths_ref)
    mask = rows_equal(docs, docs[1], HEAD_DIM, BF16)
    inverse = scale_ref[0]
    dots = scale_ref[1]
    for h in range(STEP_HEADS):
        cols = head_cols(h)
        gain = gain_ref[:, cols]
        normed = mixed_ref[:, cols] * inverse
        normed_ref[:, cols] = (normed * gain).astype(BF16)
        scaled = gain * grad_ref[:, cols].astype(F32)
        grad_mixed = ((scaled - normed * dots) * inverse).astype(BF16)
        grad_mixed_ref[:, cols] = grad_mixed
        upper_ref[h * HEAD_DIM : (h + 1) * HEAD_DIM, :] = dot(
            query_ref[:, cols] * mask, grad_mixed, TN
        )


def back_kernel(
    lengths_ref,
    query_ref,
    key_ref,
    value_ref,
    grad_ref,
    state_ref,
    query_out_ref,
    key_out_ref,
    value_out_ref,
    mask_ref,
):
    docs = grain_docs(lengths_ref)

    @pl.when(pl.program_id(0) == 0)
    def _():
        mask_ref[...] = pair_mask(docs)

    follows = rows_equal(docs, docs[0], HEAD_DIM, BF16)
    for h in range(STEP_HEADS):
        cols = head_cols(h)
        state = split_cols(state_ref[h * HEAD_DIM : (h + 1) * HEAD_DIM, :])
        from_state = dot(twice(grad_ref[:, cols] * follows), state, NT)
        for r in range(2):
            rows = slice(r * HALF, (r + 1) * HALF)
            upto = (r + 1) * HALF
            mask = mask_ref[rows, :upto]
            weights = dot(query_ref[rows, cols], key_ref[:upto, cols], NT).astype(BF16) * mask
            grads = dot(grad_ref[rows, cols], value_ref[:upto, cols], NT).astype(BF16) * mask
            query_out_ref[rows, cols] = (
                dot(grads, key_ref[:upto, cols], NN) + from_state[rows, :]
            ).astype(BF16)
            key_part = dot(grads, query_ref[rows, cols], TN)
            value_part = dot(weights, grad_ref[rows, cols], TN)
            if r == 0:
                key_out_ref[:HALF, cols] = key_part
                value_out_ref[:HALF, cols] = value_part
            else:
                key_out_ref[:HALF, cols] += key_part[:HALF, :]
                value_out_ref[:HALF, cols] += value_part[:HALF, :]
                key_out_ref[HALF:, cols] = key_part[HALF:, :]
                value_out_ref[HALF:, cols] = value_part[HALF:, :]


def final_kernel(
    lengths_ref, key_ref, value_ref, key_part_ref, value_part_ref, upper_ref, key_out_ref, value_out_ref
):
    docs = grain_docs(lengths_ref)
    leads = rows_equal(docs, docs[GRAINS + 1], HEAD_DIM, BF16)
    for h in range(STEP_HEADS):
        cols = head_cols(h)
        upper = upper_ref[h * HEAD_DIM : (h + 1) * HEAD_DIM, :]
        from_values = dot(twice(value_ref[:, cols] * leads), split_cols(upper), NT)
        from_keys = dot(twice(key_ref[:, cols] * leads), split_rows(upper), NN)
        key_out_ref[:, cols] = (key_part_ref[:, cols] + from_values).astype(BF16)
        value_out_ref[:, cols] = (value_part_ref[:, cols] + from_keys).astype(BF16)


def on_device(queries, key_input, value_input, norm_gain, out_grad, doc_lengths):
    rows_here, width_here = queries.shape
    steps = width_here // STEP_COLS
    devices = lax.axis_size("ctx")
    state_rows = width_here

    lengths = pl.BlockSpec(memory_space=pltpu.SMEM)
    wide = pl.BlockSpec((rows_here, STEP_COLS), lambda i: (0, i))
    state = pl.BlockSpec((STEP_COLS, HEAD_DIM), lambda i: (i, 0))
    gain_spec = pl.BlockSpec((1, STEP_COLS), lambda i: (0, i))
    sums_spec = pl.BlockSpec((2, rows_here), lambda i: (0, 0))

    wide_f32 = jax.ShapeDtypeStruct((rows_here, width_here), F32)
    wide_bf16 = jax.ShapeDtypeStruct((rows_here, width_here), BF16)
    state_f32 = jax.ShapeDtypeStruct((state_rows, HEAD_DIM), F32)
    sums_f32 = jax.ShapeDtypeStruct((2, rows_here), F32)
    mask_scratch = pltpu.VMEM((BLOCK, BLOCK), BF16)

    def call(body, name, ins, outs, shapes, flops, moved, scratch=(), grid=(steps,)):
        return pl.pallas_call(
            body,
            name=name,
            grid=grid,
            in_specs=[lengths] + ins,
            out_specs=outs,
            out_shape=shapes,
            scratch_shapes=list(scratch),
            compiler_params=pltpu.CompilerParams(vmem_limit_bytes=24 << 20),
            cost_estimate=pl.CostEstimate(flops=flops, bytes_accessed=moved, transcendentals=0),
        )

    gain = norm_gain.reshape(1, width_here)
    product = 2 * rows_here * HEAD_DIM * width_here
    size = rows_here * width_here

    def exchange(parts):
        shaped = parts.reshape(devices, state_rows // devices, HEAD_DIM)
        return lax.all_to_all(shaped, "ctx", 0, 0, tiled=True)

    def scan(parts, backward):
        got = exchange(parts)
        whole = pl.BlockSpec(got.shape, lambda: (0, 0, 0))
        entries = call(
            lambda *refs: scan_kernel(*refs, backward=backward),
            "scan_back" if backward else "scan_ahead",
            [whole],
            whole,
            jax.ShapeDtypeStruct(got.shape, F32),
            2 * got.size,
            8 * got.size,
            [pltpu.SMEM((devices,), jnp.int32)],
            (),
        )(doc_lengths, got)
        return lax.all_to_all(entries, "ctx", 0, 0, tiled=True).reshape(state_rows, HEAD_DIM)

    parts = call(state_kernel, "states", [wide, wide], state, state_f32, product, 8 * size)(
        doc_lengths, key_input, value_input
    )
    local = call(
        local_kernel,
        "local_mix",
        [wide, wide, wide],
        wide,
        wide_f32,
        6 * product,
        10 * size,
        [mask_scratch],
    )(doc_lengths, queries, key_input, value_input)
    entry = scan(parts, False)
    mixed, sums = call(
        mixed_kernel,
        "mix_states",
        [wide, wide, state, wide, gain_spec],
        [wide, sums_spec],
        [wide_f32, sums_f32],
        2 * product,
        14 * size,
        [pltpu.VMEM((2, rows_here, HEAD_DIM), F32)],
    )(doc_lengths, queries, local, entry, out_grad, gain)
    others = [
        lax.ppermute(sums, "head", [(i, i ^ flip) for i in range(lax.axis_size("head"))])
        for flip in (1, 3, 2)
    ]
    normed_out, grad_mixed, upper_parts = call(
        grad_kernel,
        "norm_grad",
        [sums_spec] * 4 + [wide, wide, gain_spec, wide],
        [wide, wide, state],
        [wide_bf16, wide_bf16, state_f32],
        product,
        14 * size,
        [pltpu.VMEM((2, rows_here, HEAD_DIM), F32)],
    )(doc_lengths, sums, *others, mixed, out_grad, gain, queries)
    query_grad, key_part, value_part = call(
        back_kernel,
        "local_back",
        [wide, wide, wide, wide, state],
        [wide, wide, wide],
        [wide_bf16, wide_f32, wide_f32],
        15 * product,
        20 * size,
        [mask_scratch],
    )(doc_lengths, queries, key_input, value_input, grad_mixed, entry)
    upper = scan(upper_parts, True)
    key_grad, value_grad = call(
        final_kernel,
        "back_states",
        [wide, wide, wide, wide, state],
        [wide, wide],
        [wide_bf16, wide_bf16],
        4 * product,
        16 * size,
    )(doc_lengths, key_input, value_input, key_part, value_part, upper)
    return (normed_out, query_grad, key_grad, value_grad)


def solution(mesh):
    wide = P("ctx", "head")
    return jax.shard_map(
        on_device,
        mesh=mesh,
        in_specs=(wide, wide, wide, P("head"), wide, P()),
        out_specs=(wide, wide, wide, wide),
        check_vma=False,
    )
```

```python
import jax
import jax.numpy as jnp
from jax import lax
from jax.experimental import pallas as pl
from jax.experimental.pallas import tpu as pltpu
from jax.sharding import PartitionSpec as P

HEADS = 32
HEAD_DIM = 128
BLOCK = 512
GRAIN = 128
NDOCS = 8
GRAINS = BLOCK // GRAIN
WIDTH = HEADS * HEAD_DIM
HALF = BLOCK // 2
EPSILON = 1e-06

CORES = 2
COLUMNS = 4
ROWS = 4
FLIPS = (2, 1, 3)

F32 = jnp.float32
BF16 = jnp.bfloat16
I32 = jnp.int32

NN = ((1,), (0,))
NT = ((1,), (1,))
TN = ((0,), (0,))


def dot(a, b, dims):
    return lax.dot_general(a, b, (dims, ((), ())), preferred_element_type=F32)


def place():
    index = lax.axis_index("ctx")
    return index // (CORES * COLUMNS), (index // CORES) % COLUMNS, index % CORES


def doc_starts(lengths_ref):
    starts = [I32(0)]
    for i in range(NDOCS - 1):
        starts.append(starts[-1] + lengths_ref[i])
    return starts


def grain_docs(lengths_ref):
    total = lax.axis_size("ctx") * GRAINS
    first = lax.axis_index("ctx") * GRAINS
    starts = doc_starts(lengths_ref)
    docs = []
    for k in range(-1, GRAINS + 1):
        grain = first + k
        count = (grain >= total).astype(I32) - 1
        for s in starts:
            count = count + (s <= grain).astype(I32)
        docs.append(count)
    return docs


def unbroken(lengths_ref, first, grains, backward):
    hits = I32(0)
    for s in doc_starts(lengths_ref)[1:]:
        at = s - 1 if backward else s
        hits = hits + ((at >= first) & (at < first + grains)).astype(I32)
    return (hits == 0).astype(F32)


FROM_OWN, FROM_GOT, KEEPS, NEAR, FAR, KEEP_BLOCK = 0, 1, 2, 6, 7, 8
DIRECTION = 9
FOLLOWS = 2 * DIRECTION
FIRST = FOLLOWS + GRAINS
LEADS = FIRST + GRAINS
FLAGS = 32


def write_flags(lengths_ref, flags_ref):
    index = lax.axis_index("ctx")
    row, _, core = place()
    block_of = index - core
    width = CORES * GRAINS
    span = COLUMNS * width

    def put(at, value):
        flags_ref[at : at + 1, :] = jnp.full((1, HEAD_DIM), value, F32)

    for backward in (False, True):
        base = DIRECTION if backward else 0
        earlier = block_of + (1 if backward else 0)
        later = block_of + (0 if backward else 1)
        keep = unbroken(lengths_ref, later * GRAINS, GRAINS, backward)
        is_later = index == later
        put(base + FROM_OWN, jnp.where(is_later, 1.0, keep))
        put(base + FROM_GOT, jnp.where(is_later, keep, 1.0))
        for q in range(COLUMNS):
            first = row * span + q * width
            put(base + KEEPS + q, unbroken(lengths_ref, first, width, backward))
        behind = (ROWS - 1 - row) if backward else row
        near_row = row + 1 if backward else row - 1
        near_keep = unbroken(lengths_ref, near_row * span, span, backward)
        put(base + NEAR, (behind >= 1).astype(F32))
        put(base + FAR, (behind >= 2).astype(F32) * near_keep)
        put(base + KEEP_BLOCK, unbroken(lengths_ref, earlier * GRAINS, GRAINS, backward))
    docs = grain_docs(lengths_ref)
    for base, doc in ((FOLLOWS, docs[0]), (FIRST, docs[1]), (LEADS, docs[GRAINS + 1])):
        for g in range(GRAINS):
            put(base + g, (docs[1 + g] == doc).astype(F32))


def flag(flags_ref, at):
    return flags_ref[at : at + 1, :]


def row_mask(flags_ref, base):
    parts = [
        jnp.broadcast_to(flag(flags_ref, base + g), (GRAIN, HEAD_DIM)) for g in range(GRAINS)
    ]
    return jnp.concatenate(parts, axis=0).astype(BF16)


def rows_equal(docs, doc):
    parts = [
        jnp.full((GRAIN, HEAD_DIM), (docs[1 + g] == doc).astype(F32), F32) for g in range(GRAINS)
    ]
    return jnp.concatenate(parts, axis=0).astype(BF16)


def pair_mask(docs):
    rows = lax.broadcasted_iota(I32, (GRAIN, GRAIN), 0)
    cols = lax.broadcasted_iota(I32, (GRAIN, GRAIN), 1)
    lower = jnp.where(rows >= cols, 1.0, 0.0).astype(F32)
    out = []
    for i in range(GRAINS):
        line = []
        for j in range(GRAINS):
            if j < i:
                same = (docs[1 + i] == docs[1 + j]).astype(F32)
                line.append(jnp.full((GRAIN, GRAIN), same, F32))
            elif j == i:
                line.append(lower)
            else:
                line.append(jnp.zeros((GRAIN, GRAIN), F32))
        out.append(jnp.concatenate(line, axis=1))
    return jnp.concatenate(out, axis=0).astype(BF16)


def split(x):
    high = x.astype(BF16)
    low = (x - high.astype(F32)).astype(BF16)
    return jnp.concatenate([high, low], axis=0)


def twice(x):
    return jnp.concatenate([x, x], axis=1)


def head(k, core=None):
    if core is None:
        return slice(k * HEAD_DIM, (k + 1) * HEAD_DIM)
    return pl.ds(pl.multiple_of((core * COLUMNS + k) * HEAD_DIM, HEAD_DIM), HEAD_DIM)


def rows_of(k):
    return slice(k * HEAD_DIM, (k + 1) * HEAD_DIM)


def piece(index):
    return pl.ds(pl.multiple_of(index * HEAD_DIM, HEAD_DIM), HEAD_DIM)


def state_kernel(
    lengths_ref, key_ref, value_ref, own_ref, other_ref, flags_ref, key_buf, value_buf, sems
):
    core = lax.axis_index("ctx") % CORES
    loads = []
    for g in range(GRAINS):
        rows = slice(g * GRAIN, (g + 1) * GRAIN)
        pair = []
        for m, (source, to) in enumerate(((key_ref, key_buf), (value_ref, value_buf))):
            copy = pltpu.make_async_copy(source.at[rows], to.at[rows], sems.at[m, g])
            copy.start()
            pair.append(copy)
        loads.append(pair)
    write_flags(lengths_ref, flags_ref)
    docs = grain_docs(lengths_ref)
    for g in range(0, GRAINS, 2):
        for copy in loads[g] + loads[g + 1]:
            copy.wait()
        rows = slice(g * GRAIN, (g + 2) * GRAIN)
        parts = [
            jnp.full((GRAIN, HEAD_DIM), (docs[1 + i] == docs[GRAINS]).astype(F32), F32)
            for i in (g, g + 1)
        ]
        mask = jnp.concatenate(parts, axis=0).astype(BF16)
        for side, out_ref in ((1 - core, other_ref), (core, own_ref)):
            for k in range(COLUMNS):
                cols = head(k, side)
                state = dot(key_buf[rows, cols] * mask, value_buf[rows, cols], TN)
                if g == 0:
                    out_ref[rows_of(k), :] = state
                else:
                    out_ref[rows_of(k), :] += state


def pair_kernel(flags_ref, own_ref, got_ref, keep_ref, *send_refs, base):
    _, column, _ = place()
    from_own = flag(flags_ref, base + FROM_OWN)
    from_got = flag(flags_ref, base + FROM_GOT)
    for flip, out_ref in zip((0,) + FLIPS, (keep_ref,) + send_refs):
        rows = piece(column ^ flip)
        out_ref[...] = from_own * own_ref[rows, :] + from_got * got_ref[rows, :]


def chip_order(base):
    return list(range(COLUMNS))[:: -1 if base else 1]


def row_kernel(flags_ref, keep_ref, *refs, base):
    got_refs, (parts_ref, total_ref) = refs[: len(FLIPS)], refs[len(FLIPS) :]
    _, column, _ = place()
    for flip, in_ref in zip((0,) + FLIPS, (keep_ref,) + got_refs):
        parts_ref[piece(column ^ flip), :] = in_ref[...]
    order = chip_order(base)
    running = parts_ref[rows_of(order[0]), :]
    for q in order[1:]:
        running = parts_ref[rows_of(q), :] + flag(flags_ref, base + KEEPS + q) * running
    total_ref[...] = running


def enter_kernel(flags_ref, parts_ref, near_ref, far_ref, keep_ref, *refs, base):
    send_refs, (entries_ref,) = refs[: len(FLIPS)], refs[len(FLIPS) :]
    _, column, _ = place()
    running = flag(flags_ref, base + NEAR) * near_ref[...]
    running = running + flag(flags_ref, base + FAR) * far_ref[...]
    for q in chip_order(base):
        entries_ref[rows_of(q), :] = running
        running = parts_ref[rows_of(q), :] + flag(flags_ref, base + KEEPS + q) * running
    for flip, out_ref in zip((0,) + FLIPS, (keep_ref,) + send_refs):
        out_ref[...] = entries_ref[piece(column ^ flip), :]


def unpair_kernel(flags_ref, own_ref, got_ref, keep_ref, *refs, base):
    back_refs, (mine_ref, send_ref, whole_ref) = refs[: len(FLIPS)], refs[len(FLIPS) :]
    _, column, core = place()
    for flip, in_ref in zip((0,) + FLIPS, (keep_ref,) + back_refs):
        whole_ref[piece(column ^ flip), :] = in_ref[...]
    keep = flag(flags_ref, base + KEEP_BLOCK)
    is_earlier = (core == 1) if base else (core == 0)

    @pl.when(is_earlier)
    def _():
        mine_ref[...] = whole_ref[...]
        send_ref[...] = own_ref[...] + keep * whole_ref[...]

    @pl.when(jnp.logical_not(is_earlier))
    def _():
        mine_ref[...] = got_ref[...] + keep * whole_ref[...]
        send_ref[...] = whole_ref[...]


def mask_kernel(lengths_ref, mask_ref):
    mask_ref[...] = pair_mask(grain_docs(lengths_ref))


def local_kernel(query_ref, key_ref, value_ref, mask_ref, out_ref, *, heads):
    for n, k in enumerate(heads):
        cols = head(k)
        for r in range(2):
            rows = slice(r * HALF, (r + 1) * HALF)
            upto = (r + 1) * HALF
            weights = dot(query_ref[rows, cols], key_ref[:upto, cols], NT).astype(BF16)
            weights = weights * mask_ref[rows, :upto]
            out_ref[rows, head(n)] = dot(weights, value_ref[:upto, cols], NN)


def gather_states(own_ref, got_ref, out_ref):
    core = lax.axis_index("ctx") % CORES
    for side, in_ref in ((core, own_ref), (1 - core, got_ref)):
        for k in range(COLUMNS):
            out_ref[side * COLUMNS + k] = split(in_ref[rows_of(k), :])


def beside(state):
    return jnp.concatenate([state[:HEAD_DIM], state[HEAD_DIM:]], axis=1)


def mixed_kernel(
    flags_ref, query_ref, *refs, groups
):
    local_refs, refs = refs[:groups], refs[groups:]
    own_ref, got_ref, grad_ref, gain_ref, mixed_ref, sums_ref, states_ref = refs
    gather_states(own_ref, got_ref, states_ref)
    mask = row_mask(flags_ref, FOLLOWS)
    size = CORES * COLUMNS // groups
    squares = jnp.zeros((BLOCK, HEAD_DIM), F32)
    dots = jnp.zeros((BLOCK, HEAD_DIM), F32)
    for k in range(CORES * COLUMNS):
        cols = head(k)
        group, n = divmod(k, size)
        mixed = local_refs[group][:, head(n)] + dot(
            twice(query_ref[:, cols] * mask), states_ref[k], NN
        )
        mixed_ref[:, cols] = mixed
        squares = squares + mixed * mixed
        dots = dots + mixed * (gain_ref[:, cols] * grad_ref[:, cols].astype(F32))
    sums_ref[0:1, :] = jnp.sum(squares.T, axis=0, keepdims=True)
    sums_ref[1:2, :] = jnp.sum(dots.T, axis=0, keepdims=True)


def grad_kernel(
    flags_ref,
    sums_ref,
    sums1_ref,
    sums2_ref,
    sums3_ref,
    mixed_ref,
    grad_ref,
    gain_ref,
    query_ref,
    grad_mixed_ref,
    own_ref,
    other_ref,
    inverse_ref,
):
    core = lax.axis_index("ctx") % CORES
    total = sums_ref[...] + sums1_ref[...] + sums2_ref[...] + sums3_ref[...]
    root = jnp.sqrt(total[0:1, :] / WIDTH + EPSILON)
    over = 1.0 / root
    inverse = jnp.broadcast_to(over, (HEAD_DIM, BLOCK)).T
    inverse_ref[...] = inverse
    dots = jnp.broadcast_to(total[1:2, :] * over / WIDTH, (HEAD_DIM, BLOCK)).T
    mask = row_mask(flags_ref, FIRST)
    for side, out_ref in ((1 - core, other_ref), (core, own_ref)):
        for k in range(COLUMNS):
            cols = head(k, side)
            normed = mixed_ref[:, cols] * inverse
            scaled = gain_ref[:, cols] * grad_ref[:, cols].astype(F32)
            grad_mixed = ((scaled - normed * dots) * inverse).astype(BF16)
            grad_mixed_ref[:, cols] = grad_mixed
            out_ref[rows_of(k), :] = dot(query_ref[:, cols] * mask, grad_mixed, TN)


def normed_kernel(mixed_ref, inverse_ref, gain_ref, out_ref):
    inverse = inverse_ref[...]
    for k in range(CORES * COLUMNS):
        cols = head(k)
        out_ref[:, cols] = (mixed_ref[:, cols] * inverse * gain_ref[:, cols]).astype(BF16)


def back_kernel(
    flags_ref,
    query_ref,
    key_ref,
    value_ref,
    mask_ref,
    grad_ref,
    states_ref,
    query_out_ref,
    key_out_ref,
    value_out_ref,
    *,
    heads,
):
    follows = row_mask(flags_ref, FOLLOWS)
    for n, k in enumerate(heads):
        cols = head(k)
        to = head(n)
        from_state = dot(twice(grad_ref[:, cols] * follows), beside(states_ref[k]), NT)
        for r in range(2):
            rows = slice(r * HALF, (r + 1) * HALF)
            upto = (r + 1) * HALF
            mask = mask_ref[rows, :upto]
            weights = dot(query_ref[rows, cols], key_ref[:upto, cols], NT).astype(BF16) * mask
            grads = dot(grad_ref[rows, cols], value_ref[:upto, cols], NT).astype(BF16) * mask
            query_out_ref[rows, to] = (
                dot(grads, key_ref[:upto, cols], NN) + from_state[rows, :]
            ).astype(BF16)
            key_part = dot(grads, query_ref[rows, cols], TN)
            value_part = dot(weights, grad_ref[rows, cols], TN)
            if r == 0:
                key_out_ref[:HALF, to] = key_part
                value_out_ref[:HALF, to] = value_part
            else:
                key_out_ref[:HALF, to] += key_part[:HALF, :]
                value_out_ref[:HALF, to] += value_part[:HALF, :]
                key_out_ref[HALF:, to] = key_part[HALF:, :]
                value_out_ref[HALF:, to] = value_part[HALF:, :]


def final_kernel(flags_ref, key_ref, value_ref, *refs, groups):
    parts, refs = refs[: 3 * groups], refs[3 * groups :]
    own_ref, got_ref, query_out_ref, key_out_ref, value_out_ref = refs[:5]
    key_buf, value_buf, states_ref, sems = refs[5:]
    size = CORES * COLUMNS // groups
    copies = []

    def send(source, target, sem):
        copies.append(pltpu.make_async_copy(source, target, sem))
        copies[-1].start()

    for g in range(groups):
        cols = slice(g * size * HEAD_DIM, (g + 1) * size * HEAD_DIM)
        send(parts[3 * g], query_out_ref.at[:, cols], sems.at[2, g])
    gather_states(own_ref, got_ref, states_ref)
    leads = row_mask(flags_ref, LEADS)
    for k in range(CORES * COLUMNS):
        cols = head(k)
        group, n = divmod(k, size)
        state = states_ref[k]
        from_values = dot(twice(value_ref[:, cols] * leads), beside(state), NT)
        key_buf[:, cols] = (parts[3 * group + 1][:, head(n)] + from_values).astype(BF16)
        send(key_buf.at[:, cols], key_out_ref.at[:, cols], sems.at[0, k])
        from_keys = dot(twice(key_ref[:, cols] * leads), state, NN)
        value_buf[:, cols] = (parts[3 * group + 2][:, head(n)] + from_keys).astype(BF16)
        send(value_buf.at[:, cols], value_out_ref.at[:, cols], sems.at[1, k])
    for copy in copies:
        copy.wait()


MIX_GROUPS = 2
BACK_GROUPS = 4


def on_device(queries, key_input, value_input, norm_gain, out_grad, doc_lengths):
    rows_here, width_here = queries.shape
    heads_here = width_here // HEAD_DIM
    devices = lax.axis_size("ctx")
    half_rows = COLUMNS * HEAD_DIM

    scalars = pl.BlockSpec(memory_space=pltpu.SMEM)
    vmem = pl.BlockSpec(memory_space=pltpu.VMEM)
    hbm = pl.BlockSpec(memory_space=pltpu.HBM)

    def array(rows, cols, kind=F32):
        return jax.ShapeDtypeStruct((rows, cols), kind)

    wide_f32 = array(rows_here, width_here)
    wide_bf16 = array(rows_here, width_here, BF16)
    wide_buffer = pltpu.VMEM((rows_here, width_here), BF16)
    half = array(half_rows, HEAD_DIM)
    part = array(HEAD_DIM, HEAD_DIM)
    states = jax.ShapeDtypeStruct((heads_here, 2 * HEAD_DIM, HEAD_DIM), BF16)

    product = 2 * rows_here * HEAD_DIM * HEAD_DIM

    def call(body, name, args, shapes, flops, scratch=(), ins=None, outs=None, limit=32, **fixed):
        moved = sum(a.size * a.dtype.itemsize for a in list(args) + list(shapes))
        return pl.pallas_call(
            lambda *refs: body(*refs, **fixed),
            name=name,
            in_specs=ins or [vmem] * len(args),
            out_specs=outs or [vmem] * len(shapes),
            out_shape=list(shapes),
            scratch_shapes=list(scratch),
            compiler_params=pltpu.CompilerParams(vmem_limit_bytes=limit << 20),
            cost_estimate=pl.CostEstimate(flops=flops, bytes_accessed=moved, transcendentals=0),
        )(*args)

    gain = norm_gain.reshape(1, width_here)

    def move(values, source):
        return lax.ppermute(values, "ctx", [(source(i), i) for i in range(devices)])

    def swap(values):
        return move(values, lambda i: i ^ 1)

    def along_row(values):
        return [move(v, lambda i, f=f: i ^ (f * CORES)) for v, f in zip(values, FLIPS)]

    def beneath(after, moved, work):
        started = lax.optimization_barrier((after, *work[0]))
        done = work[1](started[1:])
        moved, done = lax.optimization_barrier((moved, done))
        return moved, done

    def scan(flags, own, other, base, works):
        tag = "back" if base else "ahead"
        row = CORES * COLUMNS
        sign = row if base else -row
        results = []
        got = swap(other)
        keep, *sends = call(
            pair_kernel, "pair_" + tag, (flags, own, got), [part] * 4, 4 * half.size, base=base
        )
        gathered, done = beneath(keep, along_row(sends), works[0])
        results.append(done)
        parts, total = call(
            row_kernel, "row_" + tag, (flags, keep, *gathered), [half, part], 2 * half.size, base=base
        )
        far = move(total, lambda i: (i + 2 * sign) % devices)
        near = move(total, lambda i: (i + sign) % devices)
        (near, far), done = beneath(parts, (near, far), works[1])
        results.append(done)
        keep, *sends = call(
            enter_kernel,
            "enter_" + tag,
            (flags, parts, near, far),
            [part] * 4,
            4 * half.size,
            [pltpu.VMEM((half_rows, HEAD_DIM), F32)],
            base=base,
        )
        back, done = beneath(keep, along_row(sends), works[2])
        results.append(done)
        mine, send = call(
            unpair_kernel,
            "unpair_" + tag,
            (flags, own, got, keep, *back),
            [half, half],
            4 * half.size,
            [pltpu.VMEM((half_rows, HEAD_DIM), F32)],
            base=base,
        )
        return mine, swap(send), results

    own, other, flags = call(
        state_kernel,
        "states",
        (doc_lengths, key_input, value_input),
        [half, half, array(FLAGS, HEAD_DIM)],
        8 * product,
        [wide_buffer, wide_buffer, pltpu.SemaphoreType.DMA((2, GRAINS))],
        [scalars, hbm, hbm],
        limit=53,
    )
    inputs = (queries, key_input, value_input)

    def mask_work(_):
        return call(
            mask_kernel,
            "pair_mask",
            (doc_lengths,),
            [jax.ShapeDtypeStruct((BLOCK, BLOCK), BF16)],
            BLOCK * BLOCK,
            ins=[scalars],
        )

    size = heads_here // MIX_GROUPS
    pair_masks = mask_work(None)

    def mix_work(g):
        def run(args):
            return call(
                local_kernel,
                "local_mix",
                args,
                [array(rows_here, size * HEAD_DIM)],
                6 * size * product,
                heads=range(g * size, (g + 1) * size),
            )

        return (*inputs, *pair_masks), run

    nothing = ((), lambda args: [])
    *entry, local = scan(flags, own, other, 0, [mix_work(0), mix_work(1), nothing])
    local = [x for done in local for x in done]
    mixed, sums, entry_states = call(
        mixed_kernel,
        "mix_states",
        (flags, queries, *local, *entry, out_grad, gain),
        [wide_f32, array(2, rows_here), states],
        16 * product,
        groups=MIX_GROUPS,
    )
    others = [
        lax.ppermute(sums, "head", [(i, i ^ flip) for i in range(lax.axis_size("head"))])
        for flip in FLIPS
    ]
    grad_mixed, own, other, inverse = call(
        grad_kernel,
        "norm_grad",
        (flags, sums, *others, mixed, out_grad, gain, queries),
        [wide_bf16, half, half, array(rows_here, HEAD_DIM)],
        8 * product,
    )
    groups = heads_here // BACK_GROUPS

    def back_work(which, normed=False):
        def run(args):
            out = []
            for g in which:
                out += call(
                    back_kernel,
                    "local_back",
                    args[:7],
                    [array(rows_here, groups * HEAD_DIM, BF16)]
                    + [array(rows_here, groups * HEAD_DIM)] * 2,
                    17 * groups * product,
                    heads=range(g * groups, (g + 1) * groups),
                )
            if normed:
                out += call(normed_kernel, "normed", args[7:], [wide_bf16], 2 * wide_f32.size)
            return out

        args = (flags, *inputs, *pair_masks, grad_mixed, entry_states)
        return args + ((mixed, inverse, gain) if normed else ()), run

    *leave, pieces = scan(
        flags, own, other, DIRECTION, [back_work((0, 1)), back_work((2,)), back_work((3,), True)]
    )
    normed_out = pieces[2].pop()
    pieces = [x for done in pieces for x in done]
    query_grad, key_grad, value_grad = call(
        final_kernel,
        "back_states",
        (flags, key_input, value_input, *pieces, *leave),
        [wide_bf16] * 3,
        32 * product,
        [
            wide_buffer,
            wide_buffer,
            pltpu.VMEM((heads_here, 2 * HEAD_DIM, HEAD_DIM), BF16),
            pltpu.SemaphoreType.DMA((3, heads_here)),
        ],
        outs=[hbm] * 3,
        groups=BACK_GROUPS,
    )
    return (normed_out, query_grad, key_grad, value_grad)


def solution(mesh):
    wide = P("ctx", "head")
    return jax.shard_map(
        on_device,
        mesh=mesh,
        in_specs=(wide, wide, wide, P("head"), wide, P()),
        out_specs=(wide, wide, wide, wide),
        check_vma=False,
    )
```

```python
import jax
import jax.numpy as jnp
from jax import lax
from jax.experimental import pallas as pl
from jax.experimental.pallas import tpu as pltpu
from jax.sharding import PartitionSpec as P

HEADS = 32
HEAD_DIM = 128
BLOCK = 512
GRAIN = 128
NDOCS = 8
GRAINS = BLOCK // GRAIN
WIDTH = HEADS * HEAD_DIM
HALF = BLOCK // 2
EPSILON = 1e-06

CORES = 2
COLUMNS = 4
ROWS = 4
FLIPS = (2, 1, 3)

F32 = jnp.float32
BF16 = jnp.bfloat16
I32 = jnp.int32

NN = ((1,), (0,))
NT = ((1,), (1,))
TN = ((0,), (0,))


def dot(a, b, dims):
    return lax.dot_general(a, b, (dims, ((), ())), preferred_element_type=F32)


def place():
    index = lax.axis_index("ctx")
    return index // (CORES * COLUMNS), (index // CORES) % COLUMNS, index % CORES


def half_kept():
    row, column, core = place()
    return (row + column + core) % CORES


def doc_starts(lengths_ref):
    starts = [I32(0)]
    for i in range(NDOCS - 1):
        starts.append(starts[-1] + lengths_ref[i])
    return starts


def grain_docs(lengths_ref):
    total = lax.axis_size("ctx") * GRAINS
    first = lax.axis_index("ctx") * GRAINS
    starts = doc_starts(lengths_ref)
    docs = []
    for k in range(-1, GRAINS + 1):
        grain = first + k
        count = (grain >= total).astype(I32) - 1
        for s in starts:
            count = count + (s <= grain).astype(I32)
        docs.append(count)
    return docs


def unbroken(lengths_ref, first, grains, backward):
    hits = I32(0)
    for s in doc_starts(lengths_ref)[1:]:
        at = s - 1 if backward else s
        hits = hits + ((at >= first) & (at < first + grains)).astype(I32)
    return (hits == 0).astype(F32)


FROM_OWN, FROM_GOT, KEEPS, NEAR, FAR, KEEP_BLOCK = 0, 1, 2, 6, 7, 8
DIRECTION = 9
FOLLOWS = 2 * DIRECTION
FIRST = FOLLOWS + GRAINS
LEADS = FIRST + GRAINS
SAME = LEADS + GRAINS
FLAGS = 40


def write_flags(lengths_ref, flags_ref):
    index = lax.axis_index("ctx")
    row, _, core = place()
    block_of = index - core
    width = CORES * GRAINS
    span = COLUMNS * width

    def put(at, value):
        flags_ref[at : at + 1, :] = jnp.full((1, HEAD_DIM), value, F32)

    for backward in (False, True):
        base = DIRECTION if backward else 0
        earlier = block_of + (1 if backward else 0)
        later = block_of + (0 if backward else 1)
        keep = unbroken(lengths_ref, later * GRAINS, GRAINS, backward)
        is_later = index == later
        put(base + FROM_OWN, jnp.where(is_later, 1.0, keep))
        put(base + FROM_GOT, jnp.where(is_later, keep, 1.0))
        for q in range(COLUMNS):
            first = row * span + q * width
            put(base + KEEPS + q, unbroken(lengths_ref, first, width, backward))
        behind = (ROWS - 1 - row) if backward else row
        near_row = row + 1 if backward else row - 1
        near_keep = unbroken(lengths_ref, near_row * span, span, backward)
        put(base + NEAR, (behind >= 1).astype(F32))
        put(base + FAR, (behind >= 2).astype(F32) * near_keep)
        put(base + KEEP_BLOCK, unbroken(lengths_ref, earlier * GRAINS, GRAINS, backward))
    docs = grain_docs(lengths_ref)
    for base, doc in ((FOLLOWS, docs[0]), (FIRST, docs[1]), (LEADS, docs[GRAINS + 1])):
        for g in range(GRAINS):
            put(base + g, (docs[1 + g] == doc).astype(F32))
    for i in range(GRAINS):
        for j in range(i):
            put(SAME + i * (i - 1) // 2 + j, (docs[1 + i] == docs[1 + j]).astype(F32))


def flag(flags_ref, at):
    return flags_ref[at : at + 1, :]


def row_mask(flags_ref, base):
    parts = [
        jnp.broadcast_to(flag(flags_ref, base + g), (GRAIN, HEAD_DIM)) for g in range(GRAINS)
    ]
    return jnp.concatenate(parts, axis=0).astype(BF16)


def pair_mask(flags_ref):
    rows = lax.broadcasted_iota(I32, (GRAIN, GRAIN), 0)
    cols = lax.broadcasted_iota(I32, (GRAIN, GRAIN), 1)
    lower = jnp.where(rows >= cols, 1.0, 0.0).astype(F32)
    out = []
    for i in range(GRAINS):
        line = []
        for j in range(GRAINS):
            if j < i:
                same = flag(flags_ref, SAME + i * (i - 1) // 2 + j)
                line.append(jnp.broadcast_to(same, (GRAIN, GRAIN)))
            elif j == i:
                line.append(lower)
            else:
                line.append(jnp.zeros((GRAIN, GRAIN), F32))
        out.append(jnp.concatenate(line, axis=1))
    return jnp.concatenate(out, axis=0).astype(BF16)


def split(x):
    high = x.astype(BF16)
    low = (x - high.astype(F32)).astype(BF16)
    return jnp.concatenate([high, low], axis=0)


def twice(x):
    return jnp.concatenate([x, x], axis=1)


def head(k, core=None):
    if core is None:
        return slice(k * HEAD_DIM, (k + 1) * HEAD_DIM)
    return pl.ds(pl.multiple_of((core * COLUMNS + k) * HEAD_DIM, HEAD_DIM), HEAD_DIM)


def rows_of(k):
    return slice(k * HEAD_DIM, (k + 1) * HEAD_DIM)


def piece(index):
    return pl.ds(pl.multiple_of(index * HEAD_DIM, HEAD_DIM), HEAD_DIM)


def state_kernel(
    given_ref, key_ref, value_ref, own_ref, other_ref, flags_ref, key_buf, value_buf, lengths_ref, sems
):
    mine = half_kept()
    read = pltpu.make_async_copy(given_ref, lengths_ref, sems.at[2, 0])
    read.start()
    loads = []
    for g in range(GRAINS):
        rows = slice(g * GRAIN, (g + 1) * GRAIN)
        pair = []
        for m, (source, to) in enumerate(((key_ref, key_buf), (value_ref, value_buf))):
            copy = pltpu.make_async_copy(source.at[rows], to.at[rows], sems.at[m, g])
            copy.start()
            pair.append(copy)
        loads.append(pair)
    read.wait()
    write_flags(lengths_ref, flags_ref)
    docs = grain_docs(lengths_ref)
    for g in range(0, GRAINS, 2):
        for copy in loads[g] + loads[g + 1]:
            copy.wait()
        rows = slice(g * GRAIN, (g + 2) * GRAIN)
        parts = [
            jnp.full((GRAIN, HEAD_DIM), (docs[1 + i] == docs[GRAINS]).astype(F32), F32)
            for i in (g, g + 1)
        ]
        mask = jnp.concatenate(parts, axis=0).astype(BF16)
        for side, out_ref in ((1 - mine, other_ref), (mine, own_ref)):
            for k in range(COLUMNS):
                cols = head(k, side)
                state = dot(key_buf[rows, cols] * mask, value_buf[rows, cols], TN)
                if g == 0:
                    out_ref[rows_of(k), :] = state
                else:
                    out_ref[rows_of(k), :] += state


def pair_kernel(flags_ref, own_ref, got_ref, keep_ref, *send_refs, base):
    _, column, _ = place()
    from_own = flag(flags_ref, base + FROM_OWN)
    from_got = flag(flags_ref, base + FROM_GOT)
    for flip, out_ref in zip((0,) + FLIPS, (keep_ref,) + send_refs):
        rows = piece(column ^ flip)
        out_ref[...] = from_own * own_ref[rows, :] + from_got * got_ref[rows, :]


def chip_order(base):
    return list(range(COLUMNS))[:: -1 if base else 1]


def row_kernel(flags_ref, keep_ref, *refs, base):
    got_refs, (parts_ref, total_ref) = refs[: len(FLIPS)], refs[len(FLIPS) :]
    _, column, _ = place()
    for flip, in_ref in zip((0,) + FLIPS, (keep_ref,) + got_refs):
        parts_ref[piece(column ^ flip), :] = in_ref[...]
    order = chip_order(base)
    running = parts_ref[rows_of(order[0]), :]
    for q in order[1:]:
        running = parts_ref[rows_of(q), :] + flag(flags_ref, base + KEEPS + q) * running
    total_ref[...] = running


def enter_kernel(flags_ref, parts_ref, near_ref, far_ref, keep_ref, *refs, base):
    send_refs, (entries_ref,) = refs[: len(FLIPS)], refs[len(FLIPS) :]
    _, column, _ = place()
    running = flag(flags_ref, base + NEAR) * near_ref[...]
    running = running + flag(flags_ref, base + FAR) * far_ref[...]
    for q in chip_order(base):
        entries_ref[rows_of(q), :] = running
        running = parts_ref[rows_of(q), :] + flag(flags_ref, base + KEEPS + q) * running
    for flip, out_ref in zip((0,) + FLIPS, (keep_ref,) + send_refs):
        out_ref[...] = entries_ref[piece(column ^ flip), :]


def unpair_kernel(flags_ref, own_ref, got_ref, keep_ref, *refs, base):
    back_refs, (mine_ref, send_ref, whole_ref) = refs[: len(FLIPS)], refs[len(FLIPS) :]
    _, column, core = place()
    for flip, in_ref in zip((0,) + FLIPS, (keep_ref,) + back_refs):
        whole_ref[piece(column ^ flip), :] = in_ref[...]
    keep = flag(flags_ref, base + KEEP_BLOCK)
    is_earlier = (core == 1) if base else (core == 0)

    @pl.when(is_earlier)
    def _():
        mine_ref[...] = whole_ref[...]
        send_ref[...] = own_ref[...] + keep * whole_ref[...]

    @pl.when(jnp.logical_not(is_earlier))
    def _():
        mine_ref[...] = got_ref[...] + keep * whole_ref[...]
        send_ref[...] = whole_ref[...]


def mask_kernel(flags_ref, mask_ref):
    mask_ref[...] = pair_mask(flags_ref)


def local_kernel(query_ref, key_ref, value_ref, mask_ref, out_ref, *, heads):
    for n, k in enumerate(heads):
        cols = head(k)
        for r in range(2):
            rows = slice(r * HALF, (r + 1) * HALF)
            upto = (r + 1) * HALF
            weights = dot(query_ref[rows, cols], key_ref[:upto, cols], NT).astype(BF16)
            weights = weights * mask_ref[rows, :upto]
            out_ref[rows, head(n)] = dot(weights, value_ref[:upto, cols], NN)


def gather_states(own_ref, got_ref, out_ref):
    mine = half_kept()
    for side, in_ref in ((mine, own_ref), (1 - mine, got_ref)):
        for k in range(COLUMNS):
            out_ref[side * COLUMNS + k] = split(in_ref[rows_of(k), :])


def beside(state):
    return jnp.concatenate([state[:HEAD_DIM], state[HEAD_DIM:]], axis=1)


def mixed_kernel(
    flags_ref, query_ref, *refs, groups
):
    local_refs, refs = refs[:groups], refs[groups:]
    own_ref, got_ref, grad_ref, gain_ref, mixed_ref, sums_ref, states_ref = refs
    gather_states(own_ref, got_ref, states_ref)
    mask = row_mask(flags_ref, FOLLOWS)
    size = CORES * COLUMNS // groups
    squares = jnp.zeros((BLOCK, HEAD_DIM), F32)
    dots = jnp.zeros((BLOCK, HEAD_DIM), F32)
    for k in range(CORES * COLUMNS):
        cols = head(k)
        group, n = divmod(k, size)
        mixed = local_refs[group][:, head(n)] + dot(
            twice(query_ref[:, cols] * mask), states_ref[k], NN
        )
        mixed_ref[:, cols] = mixed
        squares = squares + mixed * mixed
        dots = dots + mixed * (gain_ref[:, cols] * grad_ref[:, cols].astype(F32))
    sums_ref[0:1, :] = jnp.sum(squares.T, axis=0, keepdims=True)
    sums_ref[1:2, :] = jnp.sum(dots.T, axis=0, keepdims=True)


def grad_kernel(
    flags_ref,
    sums_ref,
    sums1_ref,
    sums2_ref,
    sums3_ref,
    mixed_ref,
    grad_ref,
    gain_ref,
    query_ref,
    grad_mixed_ref,
    own_ref,
    other_ref,
    inverse_ref,
):
    mine = half_kept()
    total = sums_ref[...] + sums1_ref[...] + sums2_ref[...] + sums3_ref[...]
    root = jnp.sqrt(total[0:1, :] / WIDTH + EPSILON)
    over = 1.0 / root
    inverse = jnp.broadcast_to(over, (HEAD_DIM, BLOCK)).T
    inverse_ref[...] = inverse
    dots = jnp.broadcast_to(total[1:2, :] * over / WIDTH, (HEAD_DIM, BLOCK)).T
    mask = row_mask(flags_ref, FIRST)
    for side, out_ref in ((1 - mine, other_ref), (mine, own_ref)):
        for k in range(COLUMNS):
            cols = head(k, side)
            normed = mixed_ref[:, cols] * inverse
            scaled = gain_ref[:, cols] * grad_ref[:, cols].astype(F32)
            grad_mixed = ((scaled - normed * dots) * inverse).astype(BF16)
            grad_mixed_ref[:, cols] = grad_mixed
            out_ref[rows_of(k), :] = dot(query_ref[:, cols] * mask, grad_mixed, TN)


def normed_kernel(mixed_ref, inverse_ref, gain_ref, out_ref):
    inverse = inverse_ref[...]
    for k in range(CORES * COLUMNS):
        cols = head(k)
        out_ref[:, cols] = (mixed_ref[:, cols] * inverse * gain_ref[:, cols]).astype(BF16)


def back_kernel(
    flags_ref,
    query_ref,
    key_ref,
    value_ref,
    mask_ref,
    grad_ref,
    states_ref,
    query_out_ref,
    key_out_ref,
    value_out_ref,
    *,
    heads,
):
    follows = row_mask(flags_ref, FOLLOWS)
    for n, k in enumerate(heads):
        cols = head(k)
        to = head(n)
        from_state = dot(twice(grad_ref[:, cols] * follows), beside(states_ref[k]), NT)
        for r in range(2):
            rows = slice(r * HALF, (r + 1) * HALF)
            upto = (r + 1) * HALF
            mask = mask_ref[rows, :upto]
            weights = dot(query_ref[rows, cols], key_ref[:upto, cols], NT).astype(BF16) * mask
            grads = dot(grad_ref[rows, cols], value_ref[:upto, cols], NT).astype(BF16) * mask
            query_out_ref[rows, to] = (
                dot(grads, key_ref[:upto, cols], NN) + from_state[rows, :]
            ).astype(BF16)
            key_part = dot(grads, query_ref[rows, cols], TN)
            value_part = dot(weights, grad_ref[rows, cols], TN)
            if r == 0:
                key_out_ref[:HALF, to] = key_part
                value_out_ref[:HALF, to] = value_part
            else:
                key_out_ref[:HALF, to] += key_part[:HALF, :]
                value_out_ref[:HALF, to] += value_part[:HALF, :]
                key_out_ref[HALF:, to] = key_part[HALF:, :]
                value_out_ref[HALF:, to] = value_part[HALF:, :]


def store_kernel(*refs):
    parts, (out_ref, sems) = refs[:-2], refs[-2:]
    copies = []
    for g, part_ref in enumerate(parts):
        width = part_ref.shape[1]
        to = out_ref.at[:, g * width : (g + 1) * width]
        copies.append(pltpu.make_async_copy(part_ref, to, sems.at[g]))
        copies[-1].start()
    for copy in copies:
        copy.wait()


def final_kernel(flags_ref, key_ref, value_ref, *refs, groups):
    parts, refs = refs[: 2 * groups], refs[2 * groups :]
    own_ref, got_ref, key_out_ref, value_out_ref = refs[:4]
    key_buf, value_buf, states_ref, sems = refs[4:]
    size = CORES * COLUMNS // groups
    copies = []

    def send(source, target, sem):
        copies.append(pltpu.make_async_copy(source, target, sem))
        copies[-1].start()

    gather_states(own_ref, got_ref, states_ref)
    leads = row_mask(flags_ref, LEADS)
    for k in range(CORES * COLUMNS):
        cols = head(k)
        group, n = divmod(k, size)
        state = states_ref[k]
        from_values = dot(twice(value_ref[:, cols] * leads), beside(state), NT)
        key_buf[:, cols] = (parts[2 * group][:, head(n)] + from_values).astype(BF16)
        send(key_buf.at[:, cols], key_out_ref.at[:, cols], sems.at[0, k])
        from_keys = dot(twice(key_ref[:, cols] * leads), state, NN)
        value_buf[:, cols] = (parts[2 * group + 1][:, head(n)] + from_keys).astype(BF16)
        send(value_buf.at[:, cols], value_out_ref.at[:, cols], sems.at[1, k])
    for copy in copies:
        copy.wait()


MIX_GROUPS = 2
BACK_GROUPS = 4


def on_device(queries, key_input, value_input, norm_gain, out_grad, doc_lengths):
    rows_here, width_here = queries.shape
    heads_here = width_here // HEAD_DIM
    devices = lax.axis_size("ctx")
    half_rows = COLUMNS * HEAD_DIM

    vmem = pl.BlockSpec(memory_space=pltpu.VMEM)
    hbm = pl.BlockSpec(memory_space=pltpu.HBM)

    def array(rows, cols, kind=F32):
        return jax.ShapeDtypeStruct((rows, cols), kind)

    wide_f32 = array(rows_here, width_here)
    wide_bf16 = array(rows_here, width_here, BF16)
    wide_buffer = pltpu.VMEM((rows_here, width_here), BF16)
    half = array(half_rows, HEAD_DIM)
    part = array(HEAD_DIM, HEAD_DIM)
    states = jax.ShapeDtypeStruct((heads_here, 2 * HEAD_DIM, HEAD_DIM), BF16)

    product = 2 * rows_here * HEAD_DIM * HEAD_DIM

    def call(body, name, args, shapes, flops, scratch=(), ins=None, outs=None, limit=32, **fixed):
        moved = sum(a.size * a.dtype.itemsize for a in list(args) + list(shapes))
        return pl.pallas_call(
            lambda *refs: body(*refs, **fixed),
            name=name,
            in_specs=ins or [vmem] * len(args),
            out_specs=outs or [vmem] * len(shapes),
            out_shape=list(shapes),
            scratch_shapes=list(scratch),
            compiler_params=pltpu.CompilerParams(vmem_limit_bytes=limit << 20),
            cost_estimate=pl.CostEstimate(flops=flops, bytes_accessed=moved, transcendentals=0),
        )(*args)

    gain = norm_gain.reshape(1, width_here)

    def move(values, source):
        return lax.ppermute(values, "ctx", [(source(i), i) for i in range(devices)])

    def swap(values):
        return move(values, lambda i: i ^ 1)

    def along_row(values):
        return [
            move(v, lambda i, f=f: i ^ (f * CORES) ^ (f % CORES)) for v, f in zip(values, FLIPS)
        ]

    def beneath(after, moved, work):
        started = lax.optimization_barrier((after, *work[0]))
        done = work[1](started[1:])
        moved, done = lax.optimization_barrier((moved, done))
        return moved, done

    def scan(flags, own, other, base, works):
        tag = "back" if base else "ahead"
        row = CORES * COLUMNS
        sign = row if base else -row
        results = []
        got = swap(other)
        keep, *sends = call(
            pair_kernel, "pair_" + tag, (flags, own, got), [part] * 4, 4 * half.size, base=base
        )
        gathered, done = beneath(keep, along_row(sends), works[0])
        results.append(done)
        parts, total = call(
            row_kernel, "row_" + tag, (flags, keep, *gathered), [half, part], 2 * half.size, base=base
        )
        far = move(total, lambda i: (i + 2 * sign) % devices)
        near = move(total, lambda i: (i + sign) % devices ^ 1)
        (near, far), done = beneath(parts, (near, far), works[1])
        results.append(done)
        keep, *sends = call(
            enter_kernel,
            "enter_" + tag,
            (flags, parts, near, far),
            [part] * 4,
            4 * half.size,
            [pltpu.VMEM((half_rows, HEAD_DIM), F32)],
            base=base,
        )
        back, done = beneath(keep, along_row(sends), works[2])
        results.append(done)
        mine, send = call(
            unpair_kernel,
            "unpair_" + tag,
            (flags, own, got, keep, *back),
            [half, half],
            4 * half.size,
            [pltpu.VMEM((half_rows, HEAD_DIM), F32)],
            base=base,
        )
        met, done = beneath(send, swap(send), works[3])
        results.append(done)
        return mine, met, results

    own, other, flags, keys, values = call(
        state_kernel,
        "states",
        (doc_lengths, key_input, value_input),
        [half, half, array(FLAGS, HEAD_DIM), wide_bf16, wide_bf16],
        8 * product,
        [pltpu.SMEM((NDOCS,), I32), pltpu.SemaphoreType.DMA((3, GRAINS))],
        [hbm, hbm, hbm],
        limit=51,
    )
    inputs = (queries, keys, values)

    def mask_work(_):
        return call(
            mask_kernel,
            "pair_mask",
            (flags,),
            [jax.ShapeDtypeStruct((BLOCK, BLOCK), BF16)],
            BLOCK * BLOCK,
        )

    size = heads_here // MIX_GROUPS
    pair_masks = mask_work(None)

    def mix_work(g):
        def run(args):
            return call(
                local_kernel,
                "local_mix",
                args,
                [array(rows_here, size * HEAD_DIM)],
                6 * size * product,
                heads=range(g * size, (g + 1) * size),
            )

        return (*inputs, *pair_masks), run

    nothing = ((), lambda args: [])
    *entry, local = scan(flags, own, other, 0, [mix_work(0), mix_work(1), nothing, nothing])
    local = [x for done in local for x in done]
    mixed, sums, entry_states = call(
        mixed_kernel,
        "mix_states",
        (flags, queries, *local, *entry, out_grad, gain),
        [wide_f32, array(2, rows_here), states],
        16 * product,
        groups=MIX_GROUPS,
    )
    others = [
        lax.ppermute(sums, "head", [(i, i ^ flip) for i in range(lax.axis_size("head"))])
        for flip in FLIPS
    ]
    grad_mixed, own, other, inverse = call(
        grad_kernel,
        "norm_grad",
        (flags, sums, *others, mixed, out_grad, gain, queries),
        [wide_bf16, half, half, array(rows_here, HEAD_DIM)],
        8 * product,
    )
    groups = heads_here // BACK_GROUPS

    back_args = (flags, *inputs, *pair_masks, grad_mixed, entry_states)
    query_parts, pieces = [], []

    def back_work(which):
        def run(args):
            for g in which:
                query_part, *rest = call(
                    back_kernel,
                    "local_back",
                    args,
                    [array(rows_here, groups * HEAD_DIM, BF16)]
                    + [array(rows_here, groups * HEAD_DIM)] * 2,
                    17 * groups * product,
                    heads=range(g * groups, (g + 1) * groups),
                )
                query_parts.append(query_part)
                pieces.extend(rest)
            return query_parts[-len(which) :], pieces[-2 * len(which) :]

        return back_args, run

    def first_work(args):
        done = back_work((0,))[1](args[:-3])
        return done, call(normed_kernel, "normed", args[-3:], [wide_bf16], 2 * wide_f32.size)

    def store_work(_):
        return call(
            store_kernel,
            "store",
            query_parts,
            [wide_bf16],
            wide_f32.size,
            [pltpu.SemaphoreType.DMA((BACK_GROUPS,))],
            outs=[hbm],
        )

    *leave, results = scan(
        flags,
        own,
        other,
        DIRECTION,
        [
            (back_args + (mixed, inverse, gain), first_work),
            back_work((1, 2)),
            back_work((3,)),
            ((), store_work),
        ],
    )
    (first, (normed_out,)), second, third, (query_grad,) = results
    pieces = [x for done in (first, second, third) for x in done[1]]
    key_grad, value_grad = call(
        final_kernel,
        "back_states",
        (flags, keys, values, *pieces, *leave),
        [wide_bf16] * 2,
        32 * product,
        [
            wide_buffer,
            wide_buffer,
            pltpu.VMEM((heads_here, 2 * HEAD_DIM, HEAD_DIM), BF16),
            pltpu.SemaphoreType.DMA((2, heads_here)),
        ],
        outs=[hbm] * 2,
        groups=BACK_GROUPS,
    )
    return (normed_out, query_grad, key_grad, value_grad)


def solution(mesh):
    wide = P("ctx", "head")
    return jax.shard_map(
        on_device,
        mesh=mesh,
        in_specs=(wide, wide, wide, P("head"), wide, P()),
        out_specs=(wide, wide, wide, wide),
        check_vma=False,
    )
```

```python
import jax
import jax.numpy as jnp
from jax import lax
from jax.experimental import pallas as pl
from jax.experimental.pallas import tpu as pltpu
from jax.sharding import PartitionSpec as P

HEADS = 32
HEAD_DIM = 128
BLOCK = 512
GRAIN = 128
NDOCS = 8
GRAINS = BLOCK // GRAIN
WIDTH = HEADS * HEAD_DIM
HALF = BLOCK // 2
EPSILON = 1e-06

CORES = 2
COLUMNS = 4
ROWS = 4
FLIPS = (2, 1, 3)

F32 = jnp.float32
BF16 = jnp.bfloat16
I32 = jnp.int32

NN = ((1,), (0,))
NT = ((1,), (1,))
TN = ((0,), (0,))


def dot(a, b, dims):
    return lax.dot_general(a, b, (dims, ((), ())), preferred_element_type=F32)


def place():
    index = lax.axis_index("ctx")
    return index // (CORES * COLUMNS), (index // CORES) % COLUMNS, index % CORES


def half_kept():
    row, column, core = place()
    return (row + column + core) % CORES


def doc_starts(lengths_ref):
    starts = [I32(0)]
    for i in range(NDOCS - 1):
        starts.append(starts[-1] + lengths_ref[i])
    return starts


def grain_docs(lengths_ref):
    total = lax.axis_size("ctx") * GRAINS
    first = lax.axis_index("ctx") * GRAINS
    starts = doc_starts(lengths_ref)
    docs = []
    for k in range(-1, GRAINS + 1):
        grain = first + k
        count = (grain >= total).astype(I32) - 1
        for s in starts:
            count = count + (s <= grain).astype(I32)
        docs.append(count)
    return docs


def unbroken(lengths_ref, first, grains, backward):
    hits = I32(0)
    for s in doc_starts(lengths_ref)[1:]:
        at = s - 1 if backward else s
        hits = hits + ((at >= first) & (at < first + grains)).astype(I32)
    return (hits == 0).astype(F32)


FROM_OWN, FROM_GOT, KEEPS, NEAR, FAR, KEEP_BLOCK = 0, 1, 2, 6, 7, 8
DIRECTION = 9
FOLLOWS = 2 * DIRECTION
FIRST = FOLLOWS + GRAINS
LEADS = FIRST + GRAINS
SAME = LEADS + GRAINS
TAIL = SAME + GRAINS * (GRAINS - 1) // 2
FLAGS = 40


def write_flags(lengths_ref, flags_ref):
    index = lax.axis_index("ctx")
    row, _, core = place()
    block_of = index - core
    width = CORES * GRAINS
    span = COLUMNS * width

    def put(at, value):
        flags_ref[at : at + 1, :] = jnp.full((1, HEAD_DIM), value, F32)

    for backward in (False, True):
        base = DIRECTION if backward else 0
        earlier = block_of + (1 if backward else 0)
        later = block_of + (0 if backward else 1)
        keep = unbroken(lengths_ref, later * GRAINS, GRAINS, backward)
        is_later = index == later
        put(base + FROM_OWN, jnp.where(is_later, 1.0, keep))
        put(base + FROM_GOT, jnp.where(is_later, keep, 1.0))
        for q in range(COLUMNS):
            first = row * span + q * width
            put(base + KEEPS + q, unbroken(lengths_ref, first, width, backward))
        behind = (ROWS - 1 - row) if backward else row
        near_row = row + 1 if backward else row - 1
        near_keep = unbroken(lengths_ref, near_row * span, span, backward)
        put(base + NEAR, (behind >= 1).astype(F32))
        put(base + FAR, (behind >= 2).astype(F32) * near_keep)
        put(base + KEEP_BLOCK, unbroken(lengths_ref, earlier * GRAINS, GRAINS, backward))
    docs = grain_docs(lengths_ref)
    for base, doc in ((FOLLOWS, docs[0]), (FIRST, docs[1]), (LEADS, docs[GRAINS + 1]), (TAIL, docs[GRAINS])):
        for g in range(GRAINS):
            put(base + g, (docs[1 + g] == doc).astype(F32))
    for i in range(GRAINS):
        for j in range(i):
            put(SAME + i * (i - 1) // 2 + j, (docs[1 + i] == docs[1 + j]).astype(F32))


def flag(flags_ref, at):
    return flags_ref[at : at + 1, :]


def row_mask(flags_ref, base):
    parts = [
        jnp.broadcast_to(flag(flags_ref, base + g), (GRAIN, HEAD_DIM)) for g in range(GRAINS)
    ]
    return jnp.concatenate(parts, axis=0).astype(BF16)


def pair_mask(flags_ref):
    rows = lax.broadcasted_iota(I32, (GRAIN, GRAIN), 0)
    cols = lax.broadcasted_iota(I32, (GRAIN, GRAIN), 1)
    lower = jnp.where(rows >= cols, 1.0, 0.0).astype(F32)
    out = []
    for i in range(GRAINS):
        line = []
        for j in range(GRAINS):
            if j < i:
                same = flag(flags_ref, SAME + i * (i - 1) // 2 + j)
                line.append(jnp.broadcast_to(same, (GRAIN, GRAIN)))
            elif j == i:
                line.append(lower)
            else:
                line.append(jnp.zeros((GRAIN, GRAIN), F32))
        out.append(jnp.concatenate(line, axis=1))
    return jnp.concatenate(out, axis=0).astype(BF16)


def split(x):
    high = x.astype(BF16)
    low = (x - high.astype(F32)).astype(BF16)
    return jnp.concatenate([high, low], axis=0)


def twice(x):
    return jnp.concatenate([x, x], axis=1)


def head(k):
    return slice(k * HEAD_DIM, (k + 1) * HEAD_DIM)


def side_of(own):
    mine = half_kept()
    return mine if own else 1 - mine


def column(k, own, heads=1):
    start = (side_of(own) * COLUMNS + k) * HEAD_DIM
    return pl.ds(pl.multiple_of(start, heads * HEAD_DIM), heads * HEAD_DIM)


def rows_of(k):
    return slice(k * HEAD_DIM, (k + 1) * HEAD_DIM)


def piece(index):
    return pl.ds(pl.multiple_of(index * HEAD_DIM, HEAD_DIM), HEAD_DIM)


def state_kernel(
    given_ref, key_ref, value_ref, other_ref, flags_ref, key_buf, value_buf, lengths_ref, sems
):
    read = pltpu.make_async_copy(given_ref, lengths_ref, sems.at[2, 0])
    read.start()
    loads = []
    for g in range(GRAINS):
        rows = slice(g * GRAIN, (g + 1) * GRAIN)
        pair = []
        for m, (source, to) in enumerate(((key_ref, key_buf), (value_ref, value_buf))):
            copy = pltpu.make_async_copy(source.at[rows], to.at[rows], sems.at[m, g])
            copy.start()
            pair.append(copy)
        loads.append(pair)
    read.wait()
    write_flags(lengths_ref, flags_ref)
    docs = grain_docs(lengths_ref)
    for g in range(GRAINS):
        for copy in loads[g]:
            copy.wait()
        rows = slice(g * GRAIN, (g + 1) * GRAIN)
        same = (docs[1 + g] == docs[GRAINS]).astype(F32)
        mask = jnp.full((GRAIN, HEAD_DIM), same, F32).astype(BF16)
        for k in range(COLUMNS):
            cols = column(k, False)
            state = dot(key_buf[rows, cols] * mask, value_buf[rows, cols], TN)
            if g == 0:
                other_ref[rows_of(k), :] = state
            else:
                other_ref[rows_of(k), :] += state


def own_state_kernel(flags_ref, key_ref, value_ref, own_ref):
    mask = row_mask(flags_ref, TAIL)
    for k in range(COLUMNS):
        cols = column(k, True)
        own_ref[rows_of(k), :] = dot(key_ref[:, cols] * mask, value_ref[:, cols], TN)


def pair_kernel(flags_ref, own_ref, got_ref, keep_ref, *send_refs, base):
    _, at, _ = place()
    from_own = flag(flags_ref, base + FROM_OWN)
    from_got = flag(flags_ref, base + FROM_GOT)
    for flip, out_ref in zip((0,) + FLIPS, (keep_ref,) + send_refs):
        rows = piece(at ^ flip)
        out_ref[...] = from_own * own_ref[rows, :] + from_got * got_ref[rows, :]


def chip_order(base):
    return list(range(COLUMNS))[:: -1 if base else 1]


def row_kernel(flags_ref, keep_ref, *refs, base):
    got_refs, (parts_ref, total_ref) = refs[: len(FLIPS)], refs[len(FLIPS) :]
    _, at, _ = place()
    for flip, in_ref in zip((0,) + FLIPS, (keep_ref,) + got_refs):
        parts_ref[piece(at ^ flip), :] = in_ref[...]
    order = chip_order(base)
    running = parts_ref[rows_of(order[0]), :]
    for q in order[1:]:
        running = parts_ref[rows_of(q), :] + flag(flags_ref, base + KEEPS + q) * running
    total_ref[...] = running


def enter_kernel(flags_ref, parts_ref, near_ref, far_ref, keep_ref, *refs, base):
    send_refs, (entries_ref,) = refs[: len(FLIPS)], refs[len(FLIPS) :]
    _, at, _ = place()
    running = flag(flags_ref, base + NEAR) * near_ref[...]
    running = running + flag(flags_ref, base + FAR) * far_ref[...]
    for q in chip_order(base):
        entries_ref[rows_of(q), :] = running
        running = parts_ref[rows_of(q), :] + flag(flags_ref, base + KEEPS + q) * running
    for flip, out_ref in zip((0,) + FLIPS, (keep_ref,) + send_refs):
        out_ref[...] = entries_ref[piece(at ^ flip), :]


def unpair_kernel(flags_ref, own_ref, got_ref, keep_ref, *refs, base):
    back_refs, (mine_ref, send_ref, whole_ref) = refs[: len(FLIPS)], refs[len(FLIPS) :]
    _, at, core = place()
    for flip, in_ref in zip((0,) + FLIPS, (keep_ref,) + back_refs):
        whole_ref[piece(at ^ flip), :] = in_ref[...]
    keep = flag(flags_ref, base + KEEP_BLOCK)
    is_earlier = (core == 1) if base else (core == 0)

    @pl.when(is_earlier)
    def _():
        mine_ref[...] = whole_ref[...]
        send_ref[...] = own_ref[...] + keep * whole_ref[...]

    @pl.when(jnp.logical_not(is_earlier))
    def _():
        mine_ref[...] = got_ref[...] + keep * whole_ref[...]
        send_ref[...] = whole_ref[...]


def mask_kernel(flags_ref, mask_ref):
    mask_ref[...] = pair_mask(flags_ref)


def local_kernel(query_ref, key_ref, value_ref, mask_ref, out_ref, *, own):
    for k in range(COLUMNS):
        cols = column(k, own)
        for r in range(2):
            rows = slice(r * HALF, (r + 1) * HALF)
            upto = (r + 1) * HALF
            weights = dot(query_ref[rows, cols], key_ref[:upto, cols], NT).astype(BF16)
            weights = weights * mask_ref[rows, :upto]
            out_ref[rows, head(k)] = dot(weights, value_ref[:upto, cols], NN)


def beside(state):
    return jnp.concatenate([state[:HEAD_DIM], state[HEAD_DIM:]], axis=1)


def mixed_kernel(flags_ref, query_ref, local_ref, entry_ref, grad_ref, gain_ref, *refs, own):
    if own:
        mixed_ref, states_ref, squares_ref, dots_ref = refs
        squares = jnp.zeros((BLOCK, HEAD_DIM), F32)
        dots = jnp.zeros((BLOCK, HEAD_DIM), F32)
    else:
        squares_ref, dots_ref, mixed_ref, states_ref, sums_ref = refs
        squares = squares_ref[...]
        dots = dots_ref[...]
    mask = row_mask(flags_ref, FOLLOWS)
    for k in range(COLUMNS):
        cols = column(k, own)
        state = split(entry_ref[rows_of(k), :])
        states_ref[k] = state
        mixed = local_ref[:, head(k)] + dot(twice(query_ref[:, cols] * mask), state, NN)
        mixed_ref[:, head(k)] = mixed
        squares = squares + mixed * mixed
        dots = dots + mixed * (gain_ref[:, cols] * grad_ref[:, cols].astype(F32))
    if own:
        squares_ref[...] = squares
        dots_ref[...] = dots
    else:
        sums_ref[0:1, :] = jnp.sum(squares.T, axis=0, keepdims=True)
        sums_ref[1:2, :] = jnp.sum(dots.T, axis=0, keepdims=True)


def grad_kernel(flags_ref, query_ref, grad_ref, gain_ref, mixed_ref, *refs, own):
    if own:
        inverse_ref, dots_ref, grad_mixed_ref, upper_ref = refs
        inverse = inverse_ref[...]
        dots = dots_ref[...]
    else:
        sums_refs, (grad_mixed_ref, upper_ref, inverse_ref, dots_ref) = refs[:4], refs[4:]
        total = sums_refs[0][...]
        for more_ref in sums_refs[1:]:
            total = total + more_ref[...]
        over = 1.0 / jnp.sqrt(total[0:1, :] / WIDTH + EPSILON)
        inverse = jnp.broadcast_to(over, (HEAD_DIM, BLOCK)).T
        dots = jnp.broadcast_to(total[1:2, :] * over / WIDTH, (HEAD_DIM, BLOCK)).T
        inverse_ref[...] = inverse
        dots_ref[...] = dots
    mask = row_mask(flags_ref, FIRST)
    for k in range(COLUMNS):
        cols = column(k, own)
        normed = mixed_ref[:, head(k)] * inverse
        scaled = gain_ref[:, cols] * grad_ref[:, cols].astype(F32)
        grad_mixed = ((scaled - normed * dots) * inverse).astype(BF16)
        grad_mixed_ref[:, head(k)] = grad_mixed
        upper_ref[rows_of(k), :] = dot(query_ref[:, cols] * mask, grad_mixed, TN)


def normed_kernel(own_ref, other_ref, inverse_ref, gain_ref, out_ref):
    inverse = inverse_ref[...]
    for own, mixed_ref in ((True, own_ref), (False, other_ref)):
        for k in range(COLUMNS):
            cols = column(k, own)
            out_ref[:, cols] = (mixed_ref[:, head(k)] * inverse * gain_ref[:, cols]).astype(BF16)


def back_kernel(
    flags_ref,
    query_ref,
    key_ref,
    value_ref,
    mask_ref,
    grad_ref,
    states_ref,
    query_out_ref,
    key_out_ref,
    value_out_ref,
    *,
    own,
    heads,
):
    follows = row_mask(flags_ref, FOLLOWS)
    for n, k in enumerate(heads):
        cols = column(k, own)
        at = head(k)
        to = head(n)
        from_state = dot(twice(grad_ref[:, at] * follows), beside(states_ref[k]), NT)
        for r in range(2):
            rows = slice(r * HALF, (r + 1) * HALF)
            upto = (r + 1) * HALF
            mask = mask_ref[rows, :upto]
            weights = dot(query_ref[rows, cols], key_ref[:upto, cols], NT).astype(BF16) * mask
            grads = dot(grad_ref[rows, at], value_ref[:upto, cols], NT).astype(BF16) * mask
            query_out_ref[rows, to] = (
                dot(grads, key_ref[:upto, cols], NN) + from_state[rows, :]
            ).astype(BF16)
            key_part = dot(grads, query_ref[rows, cols], TN)
            value_part = dot(weights, grad_ref[rows, at], TN)
            if r == 0:
                key_out_ref[:HALF, to] = key_part
                value_out_ref[:HALF, to] = value_part
            else:
                key_out_ref[:HALF, to] += key_part[:HALF, :]
                value_out_ref[:HALF, to] += value_part[:HALF, :]
                key_out_ref[HALF:, to] = key_part[HALF:, :]
                value_out_ref[HALF:, to] = value_part[HALF:, :]


def store_kernel(*refs):
    parts, (out_ref, sems) = refs[:-2], refs[-2:]
    copies = []
    for g, part_ref in enumerate(parts):
        own = g < BACK_GROUPS // 2
        to = out_ref.at[:, column(g % (BACK_GROUPS // 2) * BACK_HEADS, own, BACK_HEADS)]
        copies.append(pltpu.make_async_copy(part_ref, to, sems.at[g]))
        copies[-1].start()
    for copy in copies:
        copy.wait()


def final_kernel(flags_ref, key_ref, value_ref, *refs, own):
    count = BACK_GROUPS // 2
    parts, (entry_ref, *refs) = refs[: 2 * count], refs[2 * count :]
    key_out_ref, value_out_ref, key_buf, value_buf, sems = refs[0 if own else 2 :]
    copies = []

    def send(source, target, sem):
        copies.append(pltpu.make_async_copy(source, target, sem))
        copies[-1].start()

    leads = row_mask(flags_ref, LEADS)
    for k in range(COLUMNS):
        cols = column(k, own)
        at = head(k)
        group, n = divmod(k, BACK_HEADS)
        state = split(entry_ref[rows_of(k), :])
        from_values = dot(twice(value_ref[:, cols] * leads), beside(state), NT)
        key_buf[:, at] = (parts[2 * group][:, head(n)] + from_values).astype(BF16)
        send(key_buf.at[:, at], key_out_ref.at[:, cols], sems.at[0, k])
        from_keys = dot(twice(key_ref[:, cols] * leads), state, NN)
        value_buf[:, at] = (parts[2 * group + 1][:, head(n)] + from_keys).astype(BF16)
        send(value_buf.at[:, at], value_out_ref.at[:, cols], sems.at[1, k])
    for copy in copies:
        copy.wait()


BACK_GROUPS = 4
BACK_HEADS = CORES * COLUMNS // BACK_GROUPS


def on_device(queries, key_input, value_input, norm_gain, out_grad, doc_lengths):
    rows_here, width_here = queries.shape
    heads_here = width_here // HEAD_DIM
    devices = lax.axis_size("ctx")
    half_rows = COLUMNS * HEAD_DIM

    vmem = pl.BlockSpec(memory_space=pltpu.VMEM)
    hbm = pl.BlockSpec(memory_space=pltpu.HBM)

    def array(rows, cols, kind=F32):
        return jax.ShapeDtypeStruct((rows, cols), kind)

    wide_f32 = array(rows_here, width_here)
    wide_bf16 = array(rows_here, width_here, BF16)
    wide_buffer = pltpu.VMEM((rows_here, width_here), BF16)
    half = array(half_rows, HEAD_DIM)
    part = array(HEAD_DIM, HEAD_DIM)
    states = jax.ShapeDtypeStruct((heads_here, 2 * HEAD_DIM, HEAD_DIM), BF16)

    product = 2 * rows_here * HEAD_DIM * HEAD_DIM

    def call(body, name, args, shapes, flops, scratch=(), ins=None, outs=None, limit=32, alias=None, **fixed):
        moved = sum(a.size * a.dtype.itemsize for a in [*args, *shapes])
        return pl.pallas_call(
            lambda *refs: body(*refs, **fixed),
            name=name,
            in_specs=ins or [vmem] * len(args),
            out_specs=outs or [vmem] * len(shapes),
            out_shape=list(shapes),
            scratch_shapes=list(scratch),
            input_output_aliases=alias or {},
            compiler_params=pltpu.CompilerParams(vmem_limit_bytes=limit << 20),
            cost_estimate=pl.CostEstimate(flops=flops, bytes_accessed=moved, transcendentals=0),
        )(*args)

    gain = norm_gain.reshape(1, width_here)

    def move(values, source):
        return lax.ppermute(values, "ctx", [(source(i), i) for i in range(devices)])

    def swap(values):
        return move(values, lambda i: i ^ 1)

    def along_row(values):
        return [
            move(v, lambda i, f=f: i ^ (f * CORES) ^ (f % CORES)) for v, f in zip(values, FLIPS)
        ]

    def beneath(after, moved, work):
        started = lax.optimization_barrier((after, *work[0]))
        done = work[1](started[1:])
        moved, done = lax.optimization_barrier((moved, done))
        return moved, done

    def scan(flags, other, base, works):
        tag = "back" if base else "ahead"
        row = CORES * COLUMNS
        sign = row if base else -row
        results = []
        got, (own, *rest) = beneath(other, swap(other), works[0]())
        results.append(rest)
        keep, *sends = call(
            pair_kernel, "pair_" + tag, (flags, own, got), [part] * 4, 4 * half.size, base=base
        )
        gathered, done = beneath(keep, along_row(sends), works[1]())
        results.append(done)
        parts, total = call(
            row_kernel, "row_" + tag, (flags, keep, *gathered), [half, part], 2 * half.size, base=base
        )
        far = move(total, lambda i: (i + 2 * sign) % devices)
        near = move(total, lambda i: (i + sign) % devices ^ 1)
        (near, far), done = beneath(parts, (near, far), works[2]())
        results.append(done)
        keep, *sends = call(
            enter_kernel,
            "enter_" + tag,
            (flags, parts, near, far),
            [part] * 4,
            4 * half.size,
            [pltpu.VMEM((half_rows, HEAD_DIM), F32)],
            base=base,
        )
        back, done = beneath(keep, along_row(sends), works[3]())
        results.append(done)
        mine, send = call(
            unpair_kernel,
            "unpair_" + tag,
            (flags, own, got, keep, *back),
            [half, half],
            4 * half.size,
            [pltpu.VMEM((half_rows, HEAD_DIM), F32)],
            base=base,
        )
        met, done = beneath(send, swap(send), works[4](mine))
        results.append(done)
        return met, results

    other, flags, keys, values = call(
        state_kernel,
        "states",
        (doc_lengths, key_input, value_input),
        [half, array(FLAGS, HEAD_DIM), wide_bf16, wide_bf16],
        4 * product,
        [pltpu.SMEM((NDOCS,), I32), pltpu.SemaphoreType.DMA((3, GRAINS))],
        [hbm, hbm, hbm],
        limit=51,
    )
    inputs = (queries, keys, values)
    (pair_masks,) = call(
        mask_kernel,
        "pair_mask",
        (flags,),
        [jax.ShapeDtypeStruct((BLOCK, BLOCK), BF16)],
        BLOCK * BLOCK,
    )
    side_f32 = array(rows_here, COLUMNS * HEAD_DIM)
    side_bf16 = array(rows_here, COLUMNS * HEAD_DIM, BF16)
    side_states = jax.ShapeDtypeStruct((COLUMNS, 2 * HEAD_DIM, HEAD_DIM), BF16)
    column_f32 = array(rows_here, HEAD_DIM)

    def own_states(args):
        return call(own_state_kernel, "own_states", args, [half], 4 * product)

    def mix_work(own):
        def run(args):
            return call(local_kernel, "local_mix", args, [side_f32], 24 * product, own=own)

        return (*inputs, pair_masks), run

    def nothing():
        return (), lambda args: []

    local = {}

    def first_mix():
        args, run = mix_work(True)

        def keep_it(args):
            local[True] = run(args)[0]
            return [local[True]]

        return args, keep_it

    def mixed_work(mine):
        def run(args):
            return call(
                mixed_kernel,
                "mix_own",
                args,
                [side_f32, side_states, column_f32, column_f32],
                8 * product,
                own=True,
            )

        return (flags, queries, local[True], mine, out_grad, gain), run

    entry, results = scan(
        flags,
        other,
        0,
        [
            lambda: ((flags, keys, values), own_states),
            first_mix,
            lambda: mix_work(False),
            nothing,
            mixed_work,
        ],
    )
    _, _, (local_other,), _, (mixed_own, states_own, *sums_so_far) = results
    mixed_other, states_other, sums = call(
        mixed_kernel,
        "mix_states",
        (flags, queries, local_other, entry, out_grad, gain, *sums_so_far),
        [side_f32, side_states, array(2, rows_here)],
        8 * product,
        own=False,
    )
    others = [
        lax.ppermute(sums, "head", [(i, i ^ flip) for i in range(lax.axis_size("head"))])
        for flip in FLIPS
    ]
    grad_other, other, inverse, dots = call(
        grad_kernel,
        "norm_grad",
        (flags, queries, out_grad, gain, mixed_other, sums, *others),
        [side_bf16, half, column_f32, column_f32],
        4 * product,
        own=False,
    )
    made = {}
    query_parts, pieces = [], []

    def own_grad(args):
        grad_own, own = call(grad_kernel, "own_grad", args, [side_bf16, half], 4 * product, own=True)
        made[True] = grad_own
        return [own, grad_own]

    def back(own, g, args):
        first = g * BACK_HEADS
        query_part, *rest = call(
            back_kernel,
            "local_back",
            args,
            [array(rows_here, BACK_HEADS * HEAD_DIM, BF16)]
            + [array(rows_here, BACK_HEADS * HEAD_DIM)] * 2,
            17 * BACK_HEADS * product,
            own=own,
            heads=range(first, first + BACK_HEADS),
        )
        query_parts.append(query_part)
        pieces.append(rest)
        return [query_part, *rest]

    back_args = (flags, *inputs, pair_masks)

    def first_back():
        def run(args):
            done = back(True, 0, args[:7])
            return [*done, *call(normed_kernel, "normed", args[7:], [wide_bf16], 2 * wide_f32.size)]

        whole = (mixed_own, mixed_other, inverse, gain)
        return (*back_args, made[True], states_own, *whole), run

    def second_back():
        def run(args):
            return [*back(True, 1, args[:7]), *back(False, 0, (*args[:5], *args[7:]))]

        return (*back_args, made[True], states_own, grad_other, states_other), run

    def third_back():
        def run(args):
            back(False, 1, args)
            return call(
                store_kernel,
                "store",
                query_parts,
                [wide_bf16],
                wide_f32.size,
                [pltpu.SemaphoreType.DMA((BACK_GROUPS,))],
                outs=[hbm],
            )

        return (*back_args, grad_other, states_other), run

    def final(own, args, so_far=()):
        buffer = pltpu.VMEM((rows_here, COLUMNS * HEAD_DIM), BF16)
        return call(
            final_kernel,
            "own_final" if own else "back_states",
            (*args, *so_far),
            [wide_bf16] * 2,
            16 * product,
            [buffer, buffer, pltpu.SemaphoreType.DMA((2, COLUMNS))],
            ins=[vmem] * len(args) + [hbm] * len(so_far),
            outs=[hbm] * 2,
            alias={len(args) + n: n for n in range(len(so_far))},
            own=own,
        )

    def final_args(which, entry):
        return (flags, keys, values, *(x for g in which for x in pieces[g]), entry)

    leave, results = scan(
        flags,
        other,
        DIRECTION,
        [
            lambda: ((flags, queries, out_grad, gain, mixed_own, inverse, dots), own_grad),
            first_back,
            second_back,
            third_back,
            lambda mine: (final_args((0, 1), mine), lambda args: final(True, args)),
        ],
    )
    normed_out = results[1][-1]
    (query_grad,) = results[3]
    key_grad, value_grad = final(False, final_args((2, 3), leave), results[4])
    return (normed_out, query_grad, key_grad, value_grad)


def solution(mesh):
    wide = P("ctx", "head")
    return jax.shard_map(
        on_device,
        mesh=mesh,
        in_specs=(wide, wide, wide, P("head"), wide, P()),
        out_specs=(wide, wide, wide, wide),
        check_vma=False,
    )
```

```python
import jax
import jax.numpy as jnp
from jax import lax
from jax.experimental import pallas as pl
from jax.experimental.pallas import tpu as pltpu
from jax.sharding import PartitionSpec as P

HEADS = 32
HEAD_DIM = 128
BLOCK = 512
GRAIN = 128
NDOCS = 8
GRAINS = BLOCK // GRAIN
WIDTH = HEADS * HEAD_DIM
HALF = BLOCK // 2
EPSILON = 1e-06

CORES = 2
COLUMNS = 4
ROWS = 4
FLIPS = (2, 1, 3)

F32 = jnp.float32
BF16 = jnp.bfloat16
I32 = jnp.int32

NN = ((1,), (0,))
NT = ((1,), (1,))
TN = ((0,), (0,))


def dot(a, b, dims):
    return lax.dot_general(a, b, (dims, ((), ())), preferred_element_type=F32)


def place():
    index = lax.axis_index("ctx")
    return index // (CORES * COLUMNS), (index // CORES) % COLUMNS, index % CORES


def half_kept():
    row, column, core = place()
    return (row + column + core) % CORES


def doc_starts(lengths_ref):
    starts = [I32(0)]
    for i in range(NDOCS - 1):
        starts.append(starts[-1] + lengths_ref[i])
    return starts


def grain_docs(lengths_ref):
    total = lax.axis_size("ctx") * GRAINS
    first = lax.axis_index("ctx") * GRAINS
    starts = doc_starts(lengths_ref)
    docs = []
    for k in range(-1, GRAINS + 1):
        grain = first + k
        count = (grain >= total).astype(I32) - 1
        for s in starts:
            count = count + (s <= grain).astype(I32)
        docs.append(count)
    return docs


def unbroken(lengths_ref, first, grains, backward):
    hits = I32(0)
    for s in doc_starts(lengths_ref)[1:]:
        at = s - 1 if backward else s
        hits = hits + ((at >= first) & (at < first + grains)).astype(I32)
    return (hits == 0).astype(F32)


FROM_OWN, FROM_GOT, KEEPS, NEAR, FAR, KEEP_BLOCK = 0, 1, 2, 6, 7, 8
DIRECTION = 9
FOLLOWS = 2 * DIRECTION
FIRST = FOLLOWS + GRAINS
LEADS = FIRST + GRAINS
SAME = LEADS + GRAINS
TAIL = SAME + GRAINS * (GRAINS - 1) // 2
FLAGS = 40


def write_flags(lengths_ref, flags_ref):
    index = lax.axis_index("ctx")
    row, _, core = place()
    block_of = index - core
    width = CORES * GRAINS
    span = COLUMNS * width

    def put(at, value):
        flags_ref[at : at + 1, :] = jnp.full((1, HEAD_DIM), value, F32)

    for backward in (False, True):
        base = DIRECTION if backward else 0
        earlier = block_of + (1 if backward else 0)
        later = block_of + (0 if backward else 1)
        keep = unbroken(lengths_ref, later * GRAINS, GRAINS, backward)
        is_later = index == later
        put(base + FROM_OWN, jnp.where(is_later, 1.0, keep))
        put(base + FROM_GOT, jnp.where(is_later, keep, 1.0))
        for q in range(COLUMNS):
            first = row * span + q * width
            put(base + KEEPS + q, unbroken(lengths_ref, first, width, backward))
        behind = (ROWS - 1 - row) if backward else row
        near_row = row + 1 if backward else row - 1
        near_keep = unbroken(lengths_ref, near_row * span, span, backward)
        put(base + NEAR, (behind >= 1).astype(F32))
        put(base + FAR, (behind >= 2).astype(F32) * near_keep)
        put(base + KEEP_BLOCK, unbroken(lengths_ref, earlier * GRAINS, GRAINS, backward))
    docs = grain_docs(lengths_ref)
    for base, doc in ((FOLLOWS, docs[0]), (FIRST, docs[1]), (LEADS, docs[GRAINS + 1]), (TAIL, docs[GRAINS])):
        for g in range(GRAINS):
            put(base + g, (docs[1 + g] == doc).astype(F32))
    for i in range(GRAINS):
        for j in range(i):
            put(SAME + i * (i - 1) // 2 + j, (docs[1 + i] == docs[1 + j]).astype(F32))


def flag(flags_ref, at):
    return flags_ref[at : at + 1, :]


def row_mask(flags_ref, base):
    parts = [
        jnp.broadcast_to(flag(flags_ref, base + g), (GRAIN, HEAD_DIM)) for g in range(GRAINS)
    ]
    return jnp.concatenate(parts, axis=0).astype(BF16)


def pair_mask(flags_ref):
    rows = lax.broadcasted_iota(I32, (GRAIN, GRAIN), 0)
    cols = lax.broadcasted_iota(I32, (GRAIN, GRAIN), 1)
    lower = jnp.where(rows >= cols, 1.0, 0.0).astype(F32)
    out = []
    for i in range(GRAINS):
        line = []
        for j in range(GRAINS):
            if j < i:
                same = flag(flags_ref, SAME + i * (i - 1) // 2 + j)
                line.append(jnp.broadcast_to(same, (GRAIN, GRAIN)))
            elif j == i:
                line.append(lower)
            else:
                line.append(jnp.zeros((GRAIN, GRAIN), F32))
        out.append(jnp.concatenate(line, axis=1))
    return jnp.concatenate(out, axis=0).astype(BF16)


def split(x):
    high = x.astype(BF16)
    low = (x - high.astype(F32)).astype(BF16)
    return jnp.concatenate([high, low], axis=0)


def twice(x):
    return jnp.concatenate([x, x], axis=1)


def head(k):
    return slice(k * HEAD_DIM, (k + 1) * HEAD_DIM)


def side_of(own):
    mine = half_kept()
    return mine if own else 1 - mine


def column(k, own, heads=1):
    start = (side_of(own) * COLUMNS + k) * HEAD_DIM
    return pl.ds(pl.multiple_of(start, heads * HEAD_DIM), heads * HEAD_DIM)


def rows_of(k):
    return slice(k * HEAD_DIM, (k + 1) * HEAD_DIM)


def piece(index):
    return pl.ds(pl.multiple_of(index * HEAD_DIM, HEAD_DIM), HEAD_DIM)


def state_kernel(
    given_ref, key_ref, value_ref, other_ref, flags_ref, key_buf, value_buf, lengths_ref, sems
):
    read = pltpu.make_async_copy(given_ref, lengths_ref, sems.at[2, 0])
    read.start()
    loads = []
    for g in range(GRAINS):
        rows = slice(g * GRAIN, (g + 1) * GRAIN)
        pair = []
        for m, (source, to) in enumerate(((key_ref, key_buf), (value_ref, value_buf))):
            copy = pltpu.make_async_copy(source.at[rows], to.at[rows], sems.at[m, g])
            copy.start()
            pair.append(copy)
        loads.append(pair)
    read.wait()
    write_flags(lengths_ref, flags_ref)
    docs = grain_docs(lengths_ref)
    for g in range(GRAINS):
        for copy in loads[g]:
            copy.wait()
        rows = slice(g * GRAIN, (g + 1) * GRAIN)
        same = (docs[1 + g] == docs[GRAINS]).astype(F32)
        mask = jnp.full((GRAIN, HEAD_DIM), same, F32).astype(BF16)
        for k in range(COLUMNS):
            cols = column(k, False)
            state = dot(key_buf[rows, cols] * mask, value_buf[rows, cols], TN)
            if g == 0:
                other_ref[rows_of(k), :] = state
            else:
                other_ref[rows_of(k), :] += state


def own_state_kernel(flags_ref, key_ref, value_ref, own_ref):
    mask = row_mask(flags_ref, TAIL)
    for k in range(COLUMNS):
        cols = column(k, True)
        own_ref[rows_of(k), :] = dot(key_ref[:, cols] * mask, value_ref[:, cols], TN)


def pair_kernel(flags_ref, own_ref, got_ref, keep_ref, *send_refs, base):
    _, at, _ = place()
    from_own = flag(flags_ref, base + FROM_OWN)
    from_got = flag(flags_ref, base + FROM_GOT)
    for flip, out_ref in zip((0,) + FLIPS, (keep_ref,) + send_refs):
        rows = piece(at ^ flip)
        out_ref[...] = from_own * own_ref[rows, :] + from_got * got_ref[rows, :]


def chip_order(base):
    return list(range(COLUMNS))[:: -1 if base else 1]


def row_kernel(flags_ref, keep_ref, *refs, base):
    got_refs, (parts_ref, total_ref) = refs[: len(FLIPS)], refs[len(FLIPS) :]
    _, at, _ = place()
    for flip, in_ref in zip((0,) + FLIPS, (keep_ref,) + got_refs):
        parts_ref[piece(at ^ flip), :] = in_ref[...]
    order = chip_order(base)
    running = parts_ref[rows_of(order[0]), :]
    for q in order[1:]:
        running = parts_ref[rows_of(q), :] + flag(flags_ref, base + KEEPS + q) * running
    total_ref[...] = running


def enter_kernel(flags_ref, parts_ref, near_ref, far_ref, keep_ref, *refs, base):
    send_refs, (entries_ref,) = refs[: len(FLIPS)], refs[len(FLIPS) :]
    _, at, _ = place()
    running = flag(flags_ref, base + NEAR) * near_ref[...]
    running = running + flag(flags_ref, base + FAR) * far_ref[...]
    for q in chip_order(base):
        entries_ref[rows_of(q), :] = running
        running = parts_ref[rows_of(q), :] + flag(flags_ref, base + KEEPS + q) * running
    for flip, out_ref in zip((0,) + FLIPS, (keep_ref,) + send_refs):
        out_ref[...] = entries_ref[piece(at ^ flip), :]


def unpair_kernel(flags_ref, own_ref, got_ref, keep_ref, *refs, base):
    back_refs, (mine_ref, send_ref, whole_ref) = refs[: len(FLIPS)], refs[len(FLIPS) :]
    _, at, core = place()
    for flip, in_ref in zip((0,) + FLIPS, (keep_ref,) + back_refs):
        whole_ref[piece(at ^ flip), :] = in_ref[...]
    keep = flag(flags_ref, base + KEEP_BLOCK)
    is_earlier = (core == 1) if base else (core == 0)

    @pl.when(is_earlier)
    def _():
        mine_ref[...] = whole_ref[...]
        send_ref[...] = own_ref[...] + keep * whole_ref[...]

    @pl.when(jnp.logical_not(is_earlier))
    def _():
        mine_ref[...] = got_ref[...] + keep * whole_ref[...]
        send_ref[...] = whole_ref[...]


def mask_kernel(flags_ref, mask_ref):
    mask_ref[...] = pair_mask(flags_ref)


def local_kernel(query_ref, key_ref, value_ref, mask_ref, out_ref, *, own):
    for k in range(COLUMNS):
        cols = column(k, own)
        for r in range(2):
            rows = slice(r * HALF, (r + 1) * HALF)
            upto = (r + 1) * HALF
            weights = dot(query_ref[rows, cols], key_ref[:upto, cols], NT).astype(BF16)
            weights = weights * mask_ref[rows, :upto]
            out_ref[rows, head(k)] = dot(weights, value_ref[:upto, cols], NN)


def beside(state):
    return jnp.concatenate([state[:HEAD_DIM], state[HEAD_DIM:]], axis=1)


def mixed_kernel(flags_ref, query_ref, local_ref, entry_ref, grad_ref, gain_ref, *refs, own):
    if own:
        mixed_ref, states_ref, squares_ref, dots_ref = refs
        squares = jnp.zeros((BLOCK, HEAD_DIM), F32)
        dots = jnp.zeros((BLOCK, HEAD_DIM), F32)
    else:
        squares_ref, dots_ref, mixed_ref, states_ref, sums_ref = refs
        squares = squares_ref[...]
        dots = dots_ref[...]
    mask = row_mask(flags_ref, FOLLOWS)
    for k in range(COLUMNS):
        cols = column(k, own)
        state = split(entry_ref[rows_of(k), :])
        states_ref[k] = state
        mixed = local_ref[:, head(k)] + dot(twice(query_ref[:, cols] * mask), state, NN)
        mixed_ref[:, head(k)] = mixed
        squares = squares + mixed * mixed
        dots = dots + mixed * (gain_ref[:, cols] * grad_ref[:, cols].astype(F32))
    if own:
        squares_ref[...] = squares
        dots_ref[...] = dots
    else:
        sums_ref[0:1, :] = jnp.sum(squares.T, axis=0, keepdims=True)
        sums_ref[1:2, :] = jnp.sum(dots.T, axis=0, keepdims=True)


def grad_kernel(flags_ref, query_ref, grad_ref, gain_ref, mixed_ref, *refs, own):
    if own:
        inverse_ref, dots_ref, grad_mixed_ref, upper_ref = refs
        inverse = inverse_ref[...]
        dots = dots_ref[...]
    else:
        sums_refs, (grad_mixed_ref, upper_ref, inverse_ref, dots_ref) = refs[:4], refs[4:]
        total = sums_refs[0][...]
        for more_ref in sums_refs[1:]:
            total = total + more_ref[...]
        over = 1.0 / jnp.sqrt(total[0:1, :] / WIDTH + EPSILON)
        inverse = jnp.broadcast_to(over, (HEAD_DIM, BLOCK)).T
        dots = jnp.broadcast_to(total[1:2, :] * over / WIDTH, (HEAD_DIM, BLOCK)).T
        inverse_ref[...] = inverse
        dots_ref[...] = dots
    mask = row_mask(flags_ref, FIRST)
    for k in range(COLUMNS):
        cols = column(k, own)
        normed = mixed_ref[:, head(k)] * inverse
        scaled = gain_ref[:, cols] * grad_ref[:, cols].astype(F32)
        grad_mixed = ((scaled - normed * dots) * inverse).astype(BF16)
        grad_mixed_ref[:, head(k)] = grad_mixed
        upper_ref[rows_of(k), :] = dot(query_ref[:, cols] * mask, grad_mixed, TN)


def normed_kernel(mixed_ref, inverse_ref, gain_ref, *refs, own):
    out_ref, buf, sems = refs[1 if own else 0 :]
    inverse = inverse_ref[...]
    copies = []
    for k in range(COLUMNS):
        cols = column(k, own)
        buf[:, head(k)] = (mixed_ref[:, head(k)] * inverse * gain_ref[:, cols]).astype(BF16)
        copies.append(pltpu.make_async_copy(buf.at[:, head(k)], out_ref.at[:, cols], sems.at[k]))
        copies[-1].start()
    for copy in copies:
        copy.wait()


def back_kernel(
    flags_ref,
    query_ref,
    key_ref,
    value_ref,
    mask_ref,
    grad_ref,
    states_ref,
    query_out_ref,
    key_out_ref,
    value_out_ref,
    *,
    own,
    heads,
):
    follows = row_mask(flags_ref, FOLLOWS)
    for n, k in enumerate(heads):
        cols = column(k, own)
        at = head(k)
        to = head(n)
        from_state = dot(twice(grad_ref[:, at] * follows), beside(states_ref[k]), NT)
        for r in range(2):
            rows = slice(r * HALF, (r + 1) * HALF)
            upto = (r + 1) * HALF
            mask = mask_ref[rows, :upto]
            weights = dot(query_ref[rows, cols], key_ref[:upto, cols], NT).astype(BF16) * mask
            grads = dot(grad_ref[rows, at], value_ref[:upto, cols], NT).astype(BF16) * mask
            query_out_ref[rows, to] = (
                dot(grads, key_ref[:upto, cols], NN) + from_state[rows, :]
            ).astype(BF16)
            key_part = dot(grads, query_ref[rows, cols], TN)
            value_part = dot(weights, grad_ref[rows, at], TN)
            if r == 0:
                key_out_ref[:HALF, to] = key_part
                value_out_ref[:HALF, to] = value_part
            else:
                key_out_ref[:HALF, to] += key_part[:HALF, :]
                value_out_ref[:HALF, to] += value_part[:HALF, :]
                key_out_ref[HALF:, to] = key_part[HALF:, :]
                value_out_ref[HALF:, to] = value_part[HALF:, :]


def store_kernel(*refs):
    parts, (out_ref, sems) = refs[:-2], refs[-2:]
    copies = []
    for g, part_ref in enumerate(parts):
        own = g < BACK_GROUPS // 2
        to = out_ref.at[:, column(g % (BACK_GROUPS // 2) * BACK_HEADS, own, BACK_HEADS)]
        copies.append(pltpu.make_async_copy(part_ref, to, sems.at[g]))
        copies[-1].start()
    for copy in copies:
        copy.wait()


def final_kernel(flags_ref, key_ref, value_ref, *refs, own):
    count = BACK_GROUPS // 2
    parts, (entry_ref, *refs) = refs[: 2 * count], refs[2 * count :]
    key_out_ref, value_out_ref, key_buf, value_buf, sems = refs[0 if own else 2 :]
    copies = []

    def send(source, target, sem):
        copies.append(pltpu.make_async_copy(source, target, sem))
        copies[-1].start()

    leads = row_mask(flags_ref, LEADS)
    for k in range(COLUMNS):
        cols = column(k, own)
        at = head(k)
        group, n = divmod(k, BACK_HEADS)
        state = split(entry_ref[rows_of(k), :])
        from_values = dot(twice(value_ref[:, cols] * leads), beside(state), NT)
        key_buf[:, at] = (parts[2 * group][:, head(n)] + from_values).astype(BF16)
        send(key_buf.at[:, at], key_out_ref.at[:, cols], sems.at[0, k])
        from_keys = dot(twice(key_ref[:, cols] * leads), state, NN)
        value_buf[:, at] = (parts[2 * group + 1][:, head(n)] + from_keys).astype(BF16)
        send(value_buf.at[:, at], value_out_ref.at[:, cols], sems.at[1, k])
    for copy in copies:
        copy.wait()


BACK_GROUPS = 4
BACK_HEADS = CORES * COLUMNS // BACK_GROUPS


def on_device(queries, key_input, value_input, norm_gain, out_grad, doc_lengths):
    rows_here, width_here = queries.shape
    heads_here = width_here // HEAD_DIM
    devices = lax.axis_size("ctx")
    half_rows = COLUMNS * HEAD_DIM

    vmem = pl.BlockSpec(memory_space=pltpu.VMEM)
    hbm = pl.BlockSpec(memory_space=pltpu.HBM)

    def array(rows, cols, kind=F32):
        return jax.ShapeDtypeStruct((rows, cols), kind)

    wide_f32 = array(rows_here, width_here)
    wide_bf16 = array(rows_here, width_here, BF16)
    wide_buffer = pltpu.VMEM((rows_here, width_here), BF16)
    half = array(half_rows, HEAD_DIM)
    part = array(HEAD_DIM, HEAD_DIM)
    states = jax.ShapeDtypeStruct((heads_here, 2 * HEAD_DIM, HEAD_DIM), BF16)

    product = 2 * rows_here * HEAD_DIM * HEAD_DIM

    def call(body, name, args, shapes, flops, scratch=(), ins=None, outs=None, limit=32, alias=None, **fixed):
        moved = sum(a.size * a.dtype.itemsize for a in [*args, *shapes])
        return pl.pallas_call(
            lambda *refs: body(*refs, **fixed),
            name=name,
            in_specs=ins or [vmem] * len(args),
            out_specs=outs or [vmem] * len(shapes),
            out_shape=list(shapes),
            scratch_shapes=list(scratch),
            input_output_aliases=alias or {},
            compiler_params=pltpu.CompilerParams(vmem_limit_bytes=limit << 20),
            cost_estimate=pl.CostEstimate(flops=flops, bytes_accessed=moved, transcendentals=0),
        )(*args)

    gain = norm_gain.reshape(1, width_here)

    def move(values, source):
        return lax.ppermute(values, "ctx", [(source(i), i) for i in range(devices)])

    def swap(values):
        return move(values, lambda i: i ^ 1)

    def along_row(values):
        return [
            move(v, lambda i, f=f: i ^ (f * CORES) ^ (f % CORES)) for v, f in zip(values, FLIPS)
        ]

    def beneath(after, moved, work):
        started = lax.optimization_barrier((after, *work[0]))
        done = work[1](started[1:])
        moved, done = lax.optimization_barrier((moved, done))
        return moved, done

    def scan(flags, other, base, works):
        tag = "back" if base else "ahead"
        row = CORES * COLUMNS
        sign = row if base else -row
        results = []
        got, (own, *rest) = beneath(other, swap(other), works[0]())
        results.append(rest)
        keep, *sends = call(
            pair_kernel, "pair_" + tag, (flags, own, got), [part] * 4, 4 * half.size, base=base
        )
        gathered, done = beneath(keep, along_row(sends), works[1]())
        results.append(done)
        parts, total = call(
            row_kernel, "row_" + tag, (flags, keep, *gathered), [half, part], 2 * half.size, base=base
        )
        far = move(total, lambda i: (i + 2 * sign) % devices)
        near = move(total, lambda i: (i + sign) % devices ^ 1)
        (near, far), done = beneath(parts, (near, far), works[2]())
        results.append(done)
        keep, *sends = call(
            enter_kernel,
            "enter_" + tag,
            (flags, parts, near, far),
            [part] * 4,
            4 * half.size,
            [pltpu.VMEM((half_rows, HEAD_DIM), F32)],
            base=base,
        )
        back, done = beneath(keep, along_row(sends), works[3]())
        results.append(done)
        mine, send = call(
            unpair_kernel,
            "unpair_" + tag,
            (flags, own, got, keep, *back),
            [half, half],
            4 * half.size,
            [pltpu.VMEM((half_rows, HEAD_DIM), F32)],
            base=base,
        )
        met, done = beneath(send, swap(send), works[4](mine))
        results.append(done)
        return met, results

    other, flags, keys, values = call(
        state_kernel,
        "states",
        (doc_lengths, key_input, value_input),
        [half, array(FLAGS, HEAD_DIM), wide_bf16, wide_bf16],
        4 * product,
        [pltpu.SMEM((NDOCS,), I32), pltpu.SemaphoreType.DMA((3, GRAINS))],
        [hbm, hbm, hbm],
        limit=51,
    )
    inputs = (queries, keys, values)
    (pair_masks,) = call(
        mask_kernel,
        "pair_mask",
        (flags,),
        [jax.ShapeDtypeStruct((BLOCK, BLOCK), BF16)],
        BLOCK * BLOCK,
    )
    side_f32 = array(rows_here, COLUMNS * HEAD_DIM)
    side_bf16 = array(rows_here, COLUMNS * HEAD_DIM, BF16)
    side_states = jax.ShapeDtypeStruct((COLUMNS, 2 * HEAD_DIM, HEAD_DIM), BF16)
    column_f32 = array(rows_here, HEAD_DIM)

    def own_states(args):
        return call(own_state_kernel, "own_states", args, [half], 4 * product)

    def mix_work(own):
        def run(args):
            return call(local_kernel, "local_mix", args, [side_f32], 24 * product, own=own)

        return (*inputs, pair_masks), run

    def nothing():
        return (), lambda args: []

    local = {}

    def first_mix():
        args, run = mix_work(True)

        def keep_it(args):
            local[True] = run(args)[0]
            return [local[True]]

        return args, keep_it

    def mixed_work(mine):
        def run(args):
            return call(
                mixed_kernel,
                "mix_own",
                args,
                [side_f32, side_states, column_f32, column_f32],
                8 * product,
                own=True,
            )

        return (flags, queries, local[True], mine, out_grad, gain), run

    entry, results = scan(
        flags,
        other,
        0,
        [
            lambda: ((flags, keys, values), own_states),
            first_mix,
            lambda: mix_work(False),
            nothing,
            mixed_work,
        ],
    )
    _, _, (local_other,), _, (mixed_own, states_own, *sums_so_far) = results
    mixed_other, states_other, sums = call(
        mixed_kernel,
        "mix_states",
        (flags, queries, local_other, entry, out_grad, gain, *sums_so_far),
        [side_f32, side_states, array(2, rows_here)],
        8 * product,
        own=False,
    )
    others = [
        lax.ppermute(sums, "head", [(i, i ^ flip) for i in range(lax.axis_size("head"))])
        for flip in FLIPS
    ]
    grad_other, other, inverse, dots = call(
        grad_kernel,
        "norm_grad",
        (flags, queries, out_grad, gain, mixed_other, sums, *others),
        [side_bf16, half, column_f32, column_f32],
        4 * product,
        own=False,
    )
    made = {}
    query_parts, pieces = [], []

    def normed(own, args):
        return call(
            normed_kernel,
            "normed",
            args,
            [wide_bf16],
            wide_f32.size,
            [pltpu.VMEM((rows_here, COLUMNS * HEAD_DIM), BF16), pltpu.SemaphoreType.DMA((COLUMNS,))],
            ins=[vmem] * 3 + [hbm] * len(args[3:]),
            outs=[hbm],
            alias={3: 0} if own else {},
            own=own,
        )

    def own_grad(args):
        grad_own, own = call(grad_kernel, "own_grad", args, [side_bf16, half], 4 * product, own=True)
        made[True] = grad_own
        made[False] = normed(False, (mixed_other, inverse, gain))[0]
        return [own, grad_own, made[False]]

    def back(own, g, args):
        first = g * BACK_HEADS
        query_part, *rest = call(
            back_kernel,
            "local_back",
            args,
            [array(rows_here, BACK_HEADS * HEAD_DIM, BF16)]
            + [array(rows_here, BACK_HEADS * HEAD_DIM)] * 2,
            17 * BACK_HEADS * product,
            own=own,
            heads=range(first, first + BACK_HEADS),
        )
        query_parts.append(query_part)
        pieces.append(rest)
        return [query_part, *rest]

    back_args = (flags, *inputs, pair_masks)

    def first_back():
        def run(args):
            done = back(True, 0, args[:7])
            return [*done, *normed(True, args[7:])]

        whole = (mixed_own, inverse, gain, made[False])
        return (*back_args, made[True], states_own, *whole), run

    def second_back():
        def run(args):
            return [*back(True, 1, args[:7]), *back(False, 0, (*args[:5], *args[7:]))]

        return (*back_args, made[True], states_own, grad_other, states_other), run

    def third_back():
        def run(args):
            back(False, 1, args)
            return call(
                store_kernel,
                "store",
                query_parts,
                [wide_bf16],
                wide_f32.size,
                [pltpu.SemaphoreType.DMA((BACK_GROUPS,))],
                outs=[hbm],
            )

        return (*back_args, grad_other, states_other), run

    def final(own, args, so_far=()):
        buffer = pltpu.VMEM((rows_here, COLUMNS * HEAD_DIM), BF16)
        return call(
            final_kernel,
            "own_final" if own else "back_states",
            (*args, *so_far),
            [wide_bf16] * 2,
            16 * product,
            [buffer, buffer, pltpu.SemaphoreType.DMA((2, COLUMNS))],
            ins=[vmem] * len(args) + [hbm] * len(so_far),
            outs=[hbm] * 2,
            alias={len(args) + n: n for n in range(len(so_far))},
            own=own,
        )

    def final_args(which, entry):
        return (flags, keys, values, *(x for g in which for x in pieces[g]), entry)

    leave, results = scan(
        flags,
        other,
        DIRECTION,
        [
            lambda: ((flags, queries, out_grad, gain, mixed_own, inverse, dots), own_grad),
            first_back,
            second_back,
            third_back,
            lambda mine: (final_args((0, 1), mine), lambda args: final(True, args)),
        ],
    )
    normed_out = results[1][-1]
    (query_grad,) = results[3]
    key_grad, value_grad = final(False, final_args((2, 3), leave), results[4])
    return (normed_out, query_grad, key_grad, value_grad)


def solution(mesh):
    wide = P("ctx", "head")
    return jax.shard_map(
        on_device,
        mesh=mesh,
        in_specs=(wide, wide, wide, P("head"), wide, P()),
        out_specs=(wide, wide, wide, wide),
        check_vma=False,
    )
```

```python
import jax
import jax.numpy as jnp
from jax import lax
from jax.experimental import pallas as pl
from jax.experimental.pallas import tpu as pltpu
from jax.sharding import PartitionSpec as P

HEADS = 32
HEAD_DIM = 128
BLOCK = 512
GRAIN = 128
NDOCS = 8
GRAINS = BLOCK // GRAIN
WIDTH = HEADS * HEAD_DIM
HALF = BLOCK // 2
EPSILON = 1e-06

CORES = 2
COLUMNS = 4
ROWS = 4
FLIPS = (2, 1, 3)

F32 = jnp.float32
BF16 = jnp.bfloat16
I32 = jnp.int32

NN = ((1,), (0,))
NT = ((1,), (1,))
TN = ((0,), (0,))


def dot(a, b, dims):
    return lax.dot_general(a, b, (dims, ((), ())), preferred_element_type=F32)


def place():
    index = lax.axis_index("ctx")
    return index // (CORES * COLUMNS), (index // CORES) % COLUMNS, index % CORES


def half_kept():
    row, column, core = place()
    return (row + column + core) % CORES


def doc_starts(lengths_ref):
    starts = [I32(0)]
    for i in range(NDOCS - 1):
        starts.append(starts[-1] + lengths_ref[i])
    return starts


def grain_docs(lengths_ref):
    total = lax.axis_size("ctx") * GRAINS
    first = lax.axis_index("ctx") * GRAINS
    starts = doc_starts(lengths_ref)
    docs = []
    for k in range(-1, GRAINS + 1):
        grain = first + k
        count = (grain >= total).astype(I32) - 1
        for s in starts:
            count = count + (s <= grain).astype(I32)
        docs.append(count)
    return docs


def unbroken(lengths_ref, first, grains, backward):
    hits = I32(0)
    for s in doc_starts(lengths_ref)[1:]:
        at = s - 1 if backward else s
        hits = hits + ((at >= first) & (at < first + grains)).astype(I32)
    return (hits == 0).astype(F32)


FROM_OWN, FROM_GOT, KEEPS, NEAR, FAR, KEEP_BLOCK = 0, 1, 2, 6, 7, 8
DIRECTION = 9
FOLLOWS = 2 * DIRECTION
FIRST = FOLLOWS + GRAINS
LEADS = FIRST + GRAINS
SAME = LEADS + GRAINS
TAIL = SAME + GRAINS * (GRAINS - 1) // 2
FLAGS = 40


def write_flags(lengths_ref, flags_ref):
    index = lax.axis_index("ctx")
    row, _, core = place()
    block_of = index - core
    width = CORES * GRAINS
    span = COLUMNS * width

    def put(at, value):
        flags_ref[at : at + 1, :] = jnp.full((1, HEAD_DIM), value, F32)

    for backward in (False, True):
        base = DIRECTION if backward else 0
        earlier = block_of + (1 if backward else 0)
        later = block_of + (0 if backward else 1)
        keep = unbroken(lengths_ref, later * GRAINS, GRAINS, backward)
        is_later = index == later
        put(base + FROM_OWN, jnp.where(is_later, 1.0, keep))
        put(base + FROM_GOT, jnp.where(is_later, keep, 1.0))
        for q in range(COLUMNS):
            first = row * span + q * width
            put(base + KEEPS + q, unbroken(lengths_ref, first, width, backward))
        behind = (ROWS - 1 - row) if backward else row
        near_row = row + 1 if backward else row - 1
        near_keep = unbroken(lengths_ref, near_row * span, span, backward)
        put(base + NEAR, (behind >= 1).astype(F32))
        put(base + FAR, (behind >= 2).astype(F32) * near_keep)
        put(base + KEEP_BLOCK, unbroken(lengths_ref, earlier * GRAINS, GRAINS, backward))
    docs = grain_docs(lengths_ref)
    for base, doc in ((FOLLOWS, docs[0]), (FIRST, docs[1]), (LEADS, docs[GRAINS + 1]), (TAIL, docs[GRAINS])):
        for g in range(GRAINS):
            put(base + g, (docs[1 + g] == doc).astype(F32))
    for i in range(GRAINS):
        for j in range(i):
            put(SAME + i * (i - 1) // 2 + j, (docs[1 + i] == docs[1 + j]).astype(F32))


def flag(flags_ref, at):
    return flags_ref[at : at + 1, :]


def row_mask(flags_ref, base):
    parts = [
        jnp.broadcast_to(flag(flags_ref, base + g), (GRAIN, HEAD_DIM)) for g in range(GRAINS)
    ]
    return jnp.concatenate(parts, axis=0).astype(BF16)


def pair_mask(flags_ref):
    rows = lax.broadcasted_iota(I32, (GRAIN, GRAIN), 0)
    cols = lax.broadcasted_iota(I32, (GRAIN, GRAIN), 1)
    lower = jnp.where(rows >= cols, 1.0, 0.0).astype(F32)
    out = []
    for i in range(GRAINS):
        line = []
        for j in range(GRAINS):
            if j < i:
                same = flag(flags_ref, SAME + i * (i - 1) // 2 + j)
                line.append(jnp.broadcast_to(same, (GRAIN, GRAIN)))
            elif j == i:
                line.append(lower)
            else:
                line.append(jnp.zeros((GRAIN, GRAIN), F32))
        out.append(jnp.concatenate(line, axis=1))
    return jnp.concatenate(out, axis=0).astype(BF16)


def split(x):
    high = x.astype(BF16)
    low = (x - high.astype(F32)).astype(BF16)
    return jnp.concatenate([high, low], axis=0)


def twice(x):
    return jnp.concatenate([x, x], axis=1)


def head(k):
    return slice(k * HEAD_DIM, (k + 1) * HEAD_DIM)


def side_of(own):
    mine = half_kept()
    return mine if own else 1 - mine


def column(k, own, heads=1):
    start = (side_of(own) * COLUMNS + k) * HEAD_DIM
    return pl.ds(pl.multiple_of(start, heads * HEAD_DIM), heads * HEAD_DIM)


def rows_of(k):
    return slice(k * HEAD_DIM, (k + 1) * HEAD_DIM)


def piece(index):
    return pl.ds(pl.multiple_of(index * HEAD_DIM, HEAD_DIM), HEAD_DIM)


def state_kernel(
    given_ref, key_ref, value_ref, other_ref, flags_ref, key_buf, value_buf, lengths_ref, sems
):
    read = pltpu.make_async_copy(given_ref, lengths_ref, sems.at[2, 0])
    read.start()
    loads = []
    for g in range(GRAINS):
        rows = slice(g * GRAIN, (g + 1) * GRAIN)
        pair = []
        for m, (source, to) in enumerate(((key_ref, key_buf), (value_ref, value_buf))):
            copy = pltpu.make_async_copy(source.at[rows], to.at[rows], sems.at[m, g])
            copy.start()
            pair.append(copy)
        loads.append(pair)
    read.wait()
    write_flags(lengths_ref, flags_ref)
    docs = grain_docs(lengths_ref)
    for g in range(GRAINS):
        for copy in loads[g]:
            copy.wait()
        rows = slice(g * GRAIN, (g + 1) * GRAIN)
        same = (docs[1 + g] == docs[GRAINS]).astype(F32)
        mask = jnp.full((GRAIN, HEAD_DIM), same, F32).astype(BF16)
        for k in range(COLUMNS):
            cols = column(k, False)
            state = dot(key_buf[rows, cols] * mask, value_buf[rows, cols], TN)
            if g == 0:
                other_ref[rows_of(k), :] = state
            else:
                other_ref[rows_of(k), :] += state


def own_state_kernel(flags_ref, key_ref, value_ref, own_ref):
    mask = row_mask(flags_ref, TAIL)
    for k in range(COLUMNS):
        cols = column(k, True)
        own_ref[rows_of(k), :] = dot(key_ref[:, cols] * mask, value_ref[:, cols], TN)


def pair_kernel(flags_ref, own_ref, got_ref, keep_ref, *send_refs, base):
    _, at, _ = place()
    from_own = flag(flags_ref, base + FROM_OWN)
    from_got = flag(flags_ref, base + FROM_GOT)
    for flip, out_ref in zip((0,) + FLIPS, (keep_ref,) + send_refs):
        rows = piece(at ^ flip)
        out_ref[...] = from_own * own_ref[rows, :] + from_got * got_ref[rows, :]


def chip_order(base):
    return list(range(COLUMNS))[:: -1 if base else 1]


def row_kernel(flags_ref, keep_ref, *refs, base):
    got_refs, (parts_ref, total_ref) = refs[: len(FLIPS)], refs[len(FLIPS) :]
    _, at, _ = place()
    for flip, in_ref in zip((0,) + FLIPS, (keep_ref,) + got_refs):
        parts_ref[piece(at ^ flip), :] = in_ref[...]
    order = chip_order(base)
    running = parts_ref[rows_of(order[0]), :]
    for q in order[1:]:
        running = parts_ref[rows_of(q), :] + flag(flags_ref, base + KEEPS + q) * running
    total_ref[...] = running


def enter_kernel(flags_ref, parts_ref, near_ref, far_ref, keep_ref, *refs, base):
    send_refs, (entries_ref,) = refs[: len(FLIPS)], refs[len(FLIPS) :]
    _, at, _ = place()
    running = flag(flags_ref, base + NEAR) * near_ref[...]
    running = running + flag(flags_ref, base + FAR) * far_ref[...]
    for q in chip_order(base):
        entries_ref[rows_of(q), :] = running
        running = parts_ref[rows_of(q), :] + flag(flags_ref, base + KEEPS + q) * running
    for flip, out_ref in zip((0,) + FLIPS, (keep_ref,) + send_refs):
        out_ref[...] = entries_ref[piece(at ^ flip), :]


def unpair_kernel(flags_ref, own_ref, got_ref, keep_ref, *refs, base):
    back_refs, (mine_ref, send_ref, whole_ref) = refs[: len(FLIPS)], refs[len(FLIPS) :]
    _, at, core = place()
    for flip, in_ref in zip((0,) + FLIPS, (keep_ref,) + back_refs):
        whole_ref[piece(at ^ flip), :] = in_ref[...]
    keep = flag(flags_ref, base + KEEP_BLOCK)
    is_earlier = (core == 1) if base else (core == 0)

    @pl.when(is_earlier)
    def _():
        mine_ref[...] = whole_ref[...]
        send_ref[...] = own_ref[...] + keep * whole_ref[...]

    @pl.when(jnp.logical_not(is_earlier))
    def _():
        mine_ref[...] = got_ref[...] + keep * whole_ref[...]
        send_ref[...] = whole_ref[...]


def mask_kernel(flags_ref, mask_ref):
    mask_ref[...] = pair_mask(flags_ref)


def local_kernel(query_ref, key_ref, value_ref, mask_ref, out_ref, *, own):
    for k in range(COLUMNS):
        cols = column(k, own)
        for r in range(2):
            rows = slice(r * HALF, (r + 1) * HALF)
            upto = (r + 1) * HALF
            weights = dot(query_ref[rows, cols], key_ref[:upto, cols], NT).astype(BF16)
            weights = weights * mask_ref[rows, :upto]
            out_ref[rows, head(k)] = dot(weights, value_ref[:upto, cols], NN)


def beside(state):
    return jnp.concatenate([state[:HEAD_DIM], state[HEAD_DIM:]], axis=1)


def mixed_kernel(flags_ref, query_ref, local_ref, entry_ref, grad_ref, gain_ref, *refs, own):
    if own:
        mixed_ref, states_ref, squares_ref, dots_ref = refs
        squares = jnp.zeros((BLOCK, HEAD_DIM), F32)
        dots = jnp.zeros((BLOCK, HEAD_DIM), F32)
    else:
        squares_ref, dots_ref, mixed_ref, states_ref, sums_ref = refs
        squares = squares_ref[...]
        dots = dots_ref[...]
    mask = row_mask(flags_ref, FOLLOWS)
    for k in range(COLUMNS):
        cols = column(k, own)
        state = split(entry_ref[rows_of(k), :])
        states_ref[k] = state
        mixed = local_ref[:, head(k)] + dot(twice(query_ref[:, cols] * mask), state, NN)
        mixed_ref[:, head(k)] = mixed
        squares = squares + mixed * mixed
        dots = dots + mixed * (gain_ref[:, cols] * grad_ref[:, cols].astype(F32))
    if own:
        squares_ref[...] = squares
        dots_ref[...] = dots
    else:
        sums_ref[0:1, :] = jnp.sum(squares.T, axis=0, keepdims=True)
        sums_ref[1:2, :] = jnp.sum(dots.T, axis=0, keepdims=True)


def grad_kernel(flags_ref, query_ref, grad_ref, gain_ref, mixed_ref, *refs, own):
    if own:
        inverse_ref, dots_ref, grad_mixed_ref, upper_ref = refs
        inverse = inverse_ref[...]
        dots = dots_ref[...]
    else:
        sums_refs, (grad_mixed_ref, upper_ref, inverse_ref, dots_ref) = refs[:4], refs[4:]
        total = sums_refs[0][...]
        for more_ref in sums_refs[1:]:
            total = total + more_ref[...]
        over = 1.0 / jnp.sqrt(total[0:1, :] / WIDTH + EPSILON)
        inverse = jnp.broadcast_to(over, (HEAD_DIM, BLOCK)).T
        dots = jnp.broadcast_to(total[1:2, :] * over / WIDTH, (HEAD_DIM, BLOCK)).T
        inverse_ref[...] = inverse
        dots_ref[...] = dots
    mask = row_mask(flags_ref, FIRST)
    for k in range(COLUMNS):
        cols = column(k, own)
        normed = mixed_ref[:, head(k)] * inverse
        scaled = gain_ref[:, cols] * grad_ref[:, cols].astype(F32)
        grad_mixed = ((scaled - normed * dots) * inverse).astype(BF16)
        grad_mixed_ref[:, head(k)] = grad_mixed
        upper_ref[rows_of(k), :] = dot(query_ref[:, cols] * mask, grad_mixed, TN)


def normed_kernel(own_ref, other_ref, inverse_ref, gain_ref, out_ref):
    inverse = inverse_ref[...]
    for own, mixed_ref in ((True, own_ref), (False, other_ref)):
        for k in range(COLUMNS):
            cols = column(k, own)
            out_ref[:, cols] = (mixed_ref[:, head(k)] * inverse * gain_ref[:, cols]).astype(BF16)


def back_kernel(
    flags_ref,
    query_ref,
    key_ref,
    value_ref,
    mask_ref,
    grad_ref,
    states_ref,
    query_out_ref,
    key_out_ref,
    value_out_ref,
    *,
    own,
    heads,
):
    follows = row_mask(flags_ref, FOLLOWS)
    for n, k in enumerate(heads):
        cols = column(k, own)
        at = head(k)
        to = head(n)
        from_state = dot(twice(grad_ref[:, at] * follows), beside(states_ref[k]), NT)
        for r in range(2):
            rows = slice(r * HALF, (r + 1) * HALF)
            upto = (r + 1) * HALF
            mask = mask_ref[rows, :upto]
            weights = dot(query_ref[rows, cols], key_ref[:upto, cols], NT).astype(BF16) * mask
            grads = dot(grad_ref[rows, at], value_ref[:upto, cols], NT).astype(BF16) * mask
            query_out_ref[rows, to] = (
                dot(grads, key_ref[:upto, cols], NN) + from_state[rows, :]
            ).astype(BF16)
            key_part = dot(grads, query_ref[rows, cols], TN)
            value_part = dot(weights, grad_ref[rows, at], TN)
            if r == 0:
                key_out_ref[:HALF, to] = key_part
                value_out_ref[:HALF, to] = value_part
            else:
                key_out_ref[:HALF, to] += key_part[:HALF, :]
                value_out_ref[:HALF, to] += value_part[:HALF, :]
                key_out_ref[HALF:, to] = key_part[HALF:, :]
                value_out_ref[HALF:, to] = value_part[HALF:, :]


def store_kernel(*refs):
    parts, (out_ref, sems) = refs[:-2], refs[-2:]
    copies = []
    for g, part_ref in enumerate(parts):
        own = g < BACK_GROUPS // 2
        to = out_ref.at[:, column(g % (BACK_GROUPS // 2) * BACK_HEADS, own, BACK_HEADS)]
        copies.append(pltpu.make_async_copy(part_ref, to, sems.at[g]))
        copies[-1].start()
    for copy in copies:
        copy.wait()


def final_kernel(flags_ref, key_ref, value_ref, *refs, own):
    count = BACK_GROUPS // 2
    parts, (entry_ref, *refs) = refs[: 2 * count], refs[2 * count :]
    key_out_ref, value_out_ref, key_buf, value_buf, sems = refs[0 if own else 2 :]
    copies = []

    def send(source, target, sem):
        copies.append(pltpu.make_async_copy(source, target, sem))
        copies[-1].start()

    leads = row_mask(flags_ref, LEADS)
    for k in range(COLUMNS):
        cols = column(k, own)
        at = head(k)
        group, n = divmod(k, BACK_HEADS)
        state = split(entry_ref[rows_of(k), :])
        from_values = dot(twice(value_ref[:, cols] * leads), beside(state), NT)
        key_buf[:, at] = (parts[2 * group][:, head(n)] + from_values).astype(BF16)
        send(key_buf.at[:, at], key_out_ref.at[:, cols], sems.at[0, k])
        from_keys = dot(twice(key_ref[:, cols] * leads), state, NN)
        value_buf[:, at] = (parts[2 * group + 1][:, head(n)] + from_keys).astype(BF16)
        send(value_buf.at[:, at], value_out_ref.at[:, cols], sems.at[1, k])
    for copy in copies:
        copy.wait()


BACK_GROUPS = 4
BACK_HEADS = CORES * COLUMNS // BACK_GROUPS


def on_device(queries, key_input, value_input, norm_gain, out_grad, doc_lengths):
    rows_here, width_here = queries.shape
    heads_here = width_here // HEAD_DIM
    devices = lax.axis_size("ctx")
    half_rows = COLUMNS * HEAD_DIM

    vmem = pl.BlockSpec(memory_space=pltpu.VMEM)
    hbm = pl.BlockSpec(memory_space=pltpu.HBM)

    def array(rows, cols, kind=F32):
        return jax.ShapeDtypeStruct((rows, cols), kind)

    wide_f32 = array(rows_here, width_here)
    wide_bf16 = array(rows_here, width_here, BF16)
    wide_buffer = pltpu.VMEM((rows_here, width_here), BF16)
    half = array(half_rows, HEAD_DIM)
    part = array(HEAD_DIM, HEAD_DIM)
    states = jax.ShapeDtypeStruct((heads_here, 2 * HEAD_DIM, HEAD_DIM), BF16)

    product = 2 * rows_here * HEAD_DIM * HEAD_DIM

    def call(body, name, args, shapes, flops, scratch=(), ins=None, outs=None, limit=32, alias=None, **fixed):
        moved = sum(a.size * a.dtype.itemsize for a in [*args, *shapes])
        return pl.pallas_call(
            lambda *refs: body(*refs, **fixed),
            name=name,
            in_specs=ins or [vmem] * len(args),
            out_specs=outs or [vmem] * len(shapes),
            out_shape=list(shapes),
            scratch_shapes=list(scratch),
            input_output_aliases=alias or {},
            compiler_params=pltpu.CompilerParams(vmem_limit_bytes=limit << 20),
            cost_estimate=pl.CostEstimate(flops=flops, bytes_accessed=moved, transcendentals=0),
        )(*args)

    gain = norm_gain.reshape(1, width_here)

    def move(values, source):
        return lax.ppermute(values, "ctx", [(source(i), i) for i in range(devices)])

    def swap(values):
        return move(values, lambda i: i ^ 1)

    def along_row(values):
        return [
            move(v, lambda i, f=f: i ^ (f * CORES) ^ (f % CORES)) for v, f in zip(values, FLIPS)
        ]

    def beneath(after, moved, work):
        started = lax.optimization_barrier((after, *work[0]))
        done = work[1](started[1:])
        moved, done = lax.optimization_barrier((moved, done))
        return moved, done

    def scan(flags, other, base, works):
        tag = "back" if base else "ahead"
        row = CORES * COLUMNS
        sign = row if base else -row
        results = []
        got, (own, *rest) = beneath(other, swap(other), works[0]())
        results.append(rest)
        keep, *sends = call(
            pair_kernel, "pair_" + tag, (flags, own, got), [part] * 4, 4 * half.size, base=base
        )
        gathered, done = beneath(keep, along_row(sends), works[1]())
        results.append(done)
        parts, total = call(
            row_kernel, "row_" + tag, (flags, keep, *gathered), [half, part], 2 * half.size, base=base
        )
        far = move(total, lambda i: (i + 2 * sign) % devices)
        near = move(total, lambda i: (i + sign) % devices ^ 1)
        (near, far), done = beneath(parts, (near, far), works[2]())
        results.append(done)
        keep, *sends = call(
            enter_kernel,
            "enter_" + tag,
            (flags, parts, near, far),
            [part] * 4,
            4 * half.size,
            [pltpu.VMEM((half_rows, HEAD_DIM), F32)],
            base=base,
        )
        back, done = beneath(keep, along_row(sends), works[3]())
        results.append(done)
        mine, send = call(
            unpair_kernel,
            "unpair_" + tag,
            (flags, own, got, keep, *back),
            [half, half],
            4 * half.size,
            [pltpu.VMEM((half_rows, HEAD_DIM), F32)],
            base=base,
        )
        met, done = beneath(send, swap(send), works[4](mine))
        results.append(done)
        return met, results

    other, flags, keys, values = call(
        state_kernel,
        "states",
        (doc_lengths, key_input, value_input),
        [half, array(FLAGS, HEAD_DIM), wide_bf16, wide_bf16],
        4 * product,
        [pltpu.SMEM((NDOCS,), I32), pltpu.SemaphoreType.DMA((3, GRAINS))],
        [hbm, hbm, hbm],
        limit=51,
    )
    inputs = (queries, keys, values)
    (pair_masks,) = call(
        mask_kernel,
        "pair_mask",
        (flags,),
        [jax.ShapeDtypeStruct((BLOCK, BLOCK), BF16)],
        BLOCK * BLOCK,
    )
    side_f32 = array(rows_here, COLUMNS * HEAD_DIM)
    side_bf16 = array(rows_here, COLUMNS * HEAD_DIM, BF16)
    side_states = jax.ShapeDtypeStruct((COLUMNS, 2 * HEAD_DIM, HEAD_DIM), BF16)
    column_f32 = array(rows_here, HEAD_DIM)

    def own_states(args):
        return call(own_state_kernel, "own_states", args, [half], 4 * product)

    def mix_work(own):
        def run(args):
            return call(local_kernel, "local_mix", args, [side_f32], 24 * product, own=own)

        return (*inputs, pair_masks), run

    def nothing():
        return (), lambda args: []

    local = {}

    def first_mix():
        args, run = mix_work(True)

        def keep_it(args):
            local[True] = run(args)[0]
            return [local[True]]

        return args, keep_it

    def mixed_work(mine):
        def run(args):
            return call(
                mixed_kernel,
                "mix_own",
                args,
                [side_f32, side_states, column_f32, column_f32],
                8 * product,
                own=True,
            )

        return (flags, queries, local[True], mine, out_grad, gain), run

    entry, results = scan(
        flags,
        other,
        0,
        [
            lambda: ((flags, keys, values), own_states),
            first_mix,
            lambda: mix_work(False),
            nothing,
            mixed_work,
        ],
    )
    _, _, (local_other,), _, (mixed_own, states_own, *sums_so_far) = results
    mixed_other, states_other, sums = call(
        mixed_kernel,
        "mix_states",
        (flags, queries, local_other, entry, out_grad, gain, *sums_so_far),
        [side_f32, side_states, array(2, rows_here)],
        8 * product,
        own=False,
    )
    others = [
        lax.ppermute(sums, "head", [(i, i ^ flip) for i in range(lax.axis_size("head"))])
        for flip in FLIPS[::-1]
    ]
    grad_other, other, inverse, dots = call(
        grad_kernel,
        "norm_grad",
        (flags, queries, out_grad, gain, mixed_other, sums, *others),
        [side_bf16, half, column_f32, column_f32],
        4 * product,
        own=False,
    )
    made = {}
    query_parts, pieces = [], []

    def own_grad(args):
        grad_own, own = call(grad_kernel, "own_grad", args, [side_bf16, half], 4 * product, own=True)
        made[True] = grad_own
        return [own, grad_own]

    def back(own, g, args):
        first = g * BACK_HEADS
        query_part, *rest = call(
            back_kernel,
            "local_back",
            args,
            [array(rows_here, BACK_HEADS * HEAD_DIM, BF16)]
            + [array(rows_here, BACK_HEADS * HEAD_DIM)] * 2,
            17 * BACK_HEADS * product,
            own=own,
            heads=range(first, first + BACK_HEADS),
        )
        query_parts.append(query_part)
        pieces.append(rest)
        return [query_part, *rest]

    back_args = (flags, *inputs, pair_masks)

    def first_back():
        def run(args):
            done = back(True, 0, args[:7])
            return [*done, *call(normed_kernel, "normed", args[7:], [wide_bf16], 2 * wide_f32.size)]

        whole = (mixed_own, mixed_other, inverse, gain)
        return (*back_args, made[True], states_own, *whole), run

    def second_back():
        def run(args):
            return [*back(True, 1, args[:7]), *back(False, 0, (*args[:5], *args[7:]))]

        return (*back_args, made[True], states_own, grad_other, states_other), run

    def third_back():
        def run(args):
            back(False, 1, args)
            return call(
                store_kernel,
                "store",
                query_parts,
                [wide_bf16],
                wide_f32.size,
                [pltpu.SemaphoreType.DMA((BACK_GROUPS,))],
                outs=[hbm],
            )

        return (*back_args, grad_other, states_other), run

    def final(own, args, so_far=()):
        buffer = pltpu.VMEM((rows_here, COLUMNS * HEAD_DIM), BF16)
        return call(
            final_kernel,
            "own_final" if own else "back_states",
            (*args, *so_far),
            [wide_bf16] * 2,
            16 * product,
            [buffer, buffer, pltpu.SemaphoreType.DMA((2, COLUMNS))],
            ins=[vmem] * len(args) + [hbm] * len(so_far),
            outs=[hbm] * 2,
            alias={len(args) + n: n for n in range(len(so_far))},
            own=own,
        )

    def final_args(which, entry):
        return (flags, keys, values, *(x for g in which for x in pieces[g]), entry)

    leave, results = scan(
        flags,
        other,
        DIRECTION,
        [
            lambda: ((flags, queries, out_grad, gain, mixed_own, inverse, dots), own_grad),
            first_back,
            second_back,
            third_back,
            lambda mine: (final_args((0, 1), mine), lambda args: final(True, args)),
        ],
    )
    normed_out = results[1][-1]
    (query_grad,) = results[3]
    key_grad, value_grad = final(False, final_args((2, 3), leave), results[4])
    return (normed_out, query_grad, key_grad, value_grad)


def solution(mesh):
    wide = P("ctx", "head")
    return jax.shard_map(
        on_device,
        mesh=mesh,
        in_specs=(wide, wide, wide, P("head"), wide, P()),
        out_specs=(wide, wide, wide, wide),
        check_vma=False,
    )
```
